32 devices in a mesh: groups: 2 (over x), fsdp: 2 (over core), rows: 8 (over z, y).
Axes of the slice: x: 2, y: 2, z: 4, core: 2. Of those that a mesh axis runs over, the one named last changes fastest.
Arguments:
- tokens: bfloat16 [4, 128, 16, 1024], P(('groups', 'fsdp'), 'rows'), parts along dimension 0, may hold values from -6 to 6
- cell_mask: int32 [4, 128, 16], P(('groups', 'fsdp'), 'rows'), parts along dimension 0, may hold values 0 or 1
- shifts: int32 [2], replicated, may hold values from 1 to 15
- projection_in: bfloat16 [1024, 1536], P(('fsdp', 'rows')), may hold values from -2 to 2
- projection_out: bfloat16 [512, 1024], P(('fsdp', 'rows')), may hold values from -0.25 to 0.25
- cotangent: bfloat16 [4, 128, 16, 1024], P(('groups', 'fsdp'), 'rows'), parts along dimension 0, may hold values from -6 to 6
Outputs:
- output: bfloat16 [4, 128, 16, 1024], P(('groups', 'fsdp'), 'rows'), parts along dimension 0
- grad_tokens: bfloat16 [4, 128, 16, 1024], P(('groups', 'fsdp'), 'rows'), parts along dimension 0
- projection_in_grad: float32 [2048, 1536], P(('groups', 'fsdp', 'rows')), parts along dimension 0
- projection_out_grad: float32 [1024, 1024], P(('groups', 'fsdp', 'rows')), parts along dimension 0
The draws below stay inside these ranges and needn't reach their ends.
There are 2 independent parts, one for each index of `groups`. The reference program is written for one: setup_inputs(seed, part) draws one part's arguments, and reference() takes and returns one part's arrays. A program takes and returns all parts, laid end to end along the dimension named above; an argument that names none is the same for every part. Nothing has to cross between parts.
All inputs are finite; a program needn't handle non-finite values. No bound on the sum of `cell_mask` on one device may be relied on, other than what follows from the above.
Results may differ from the reference program's by a relative error of at most 0.011.
Values may be sent and summed in bfloat16 or wider, within the bound.
No kernel may reach another device: no remote copies, remote signals or barrier semaphores. Data moves between devices by JAX's collectives and lax.ppermute only.
A program may use at most 64 MiB of HBM per device.

```python
import jax
import jax.numpy as jnp
from jax import lax

D = 1024
HEADS = 8
HD = 64
WIN = 16
COLS = 16
GRID_ROWS = 128
SCENES = 2


def draw_tokens(key, part):
    full_shape = (SCENES, GRID_ROWS, COLS, D)
    key_one = jax.random.fold_in(key, 0)
    values_base = jax.random.truncated_normal(key_one, -6.0, 6.0, full_shape, jnp.float32)
    return values_base.astype(jnp.bfloat16)


def draw_projection_in(key, part):
    hidden_width = HEADS * HD
    key_one = jax.random.fold_in(key, 0)
    joined = jax.random.truncated_normal(key_one, -4.0, 4.0, (D, 3 * hidden_width), jnp.float32) * D ** (-0.5)
    return joined.astype(jnp.bfloat16)


def plant(values, rng, low, high):
    extent = values.shape
    place = [jax.random.randint(jax.random.fold_in(rng, axis), (), 0, extent[axis]) for axis in range(len(extent))]
    values = values.at[tuple(place)].set(low)
    longest = extent.index(max(extent))
    place[longest] = (place[longest] + 1) % extent[longest]
    return values.at[tuple(place)].set(high)


def levels(stream_key, shape, cuts, least, largest):
    def one(axis_at, shards_of):
        heights = jax.random.uniform(jax.random.fold_in(jax.random.fold_in(stream_key, 6), axis_at), (shards_of,), jnp.float32, least / len(cuts), largest / len(cuts))
        return jnp.repeat(jnp.exp(heights), shape[axis_at] // shards_of).reshape((-1,) + (1,) * (len(shape) - axis_at - 1))

    factor_of = one(*cuts[0])
    for cut in cuts[1:]:
        factor_of = factor_of * one(*cut)
    return factor_of


def bell_draw(key, extent, spread, bound, pieces=(), kind=jnp.bfloat16):
    gain = levels(key, extent, pieces, -0.22, 0.18) if pieces else 1.0
    entries = jax.random.normal(key, extent, jnp.float32) * spread * gain
    return jnp.minimum(jnp.maximum(entries, -bound), bound).astype(kind)


def setup_inputs(seed: int = 0, part: int = 0) -> dict:
    streams_of = jax.random.split(jax.random.key(seed), 7)
    own_keys = jax.random.split(jax.random.fold_in(streams_of[6], part), 7)
    tokens = draw_tokens(jax.random.fold_in(jax.random.fold_in(streams_of[6], part), 71), part)
    cell_mask = plant((jax.random.randint(own_keys[1], (SCENES, GRID_ROWS, COLS), 0, 4) < 3).astype(jnp.int32), jax.random.fold_in(own_keys[1], 1), 0, 1)
    shifts = jax.random.randint(streams_of[2], (2,), 1, WIN).astype(jnp.int32)
    projection_in = draw_projection_in(jax.random.fold_in(streams_of[6], 71), part)
    projection_out = bell_draw(streams_of[4], (HEADS * HD, D), (HEADS * HD) ** -0.5, 0.25, ((0, 16),))
    cotangent = bell_draw(own_keys[5], (SCENES, GRID_ROWS, COLS, D), 1.0, 6.0, ((0, 2), (1, 8)))
    return {"tokens": tokens, "cell_mask": cell_mask, "shifts": shifts, "projection_in": projection_in, "projection_out": projection_out, "cotangent": cotangent}


def roll_axis(values_in, offset, axis_index):
    length = values_in.shape[axis_index]
    doubled = jnp.concatenate([values_in, values_in], axis=axis_index)
    return lax.dynamic_slice_in_dim(doubled, offset, length, axis_index)

def group_windows(grid_field):
    scenes, grid_rows, col_count, channels = grid_field.shape
    blocks = grid_field.reshape(scenes, grid_rows // WIN, WIN, col_count // WIN, WIN, channels)
    blocks = blocks.transpose(0, 1, 3, 2, 4, 5)
    return blocks.reshape(scenes * (grid_rows // WIN), col_count // WIN, WIN * WIN, channels)

def ungroup_windows(windowed, scenes, grid_rows, col_count):
    channels = windowed.shape[-1]
    blocks = windowed.reshape(scenes, grid_rows // WIN, col_count // WIN, WIN, WIN, channels)
    blocks = blocks.transpose(0, 1, 3, 2, 4, 5)
    return blocks.reshape(scenes, grid_rows, col_count, channels)

def normalize(values_f32):
    mean_value = lax.optimization_barrier(jnp.mean(values_f32, axis=-1, keepdims=True))
    centered = values_f32 - mean_value
    variance = lax.optimization_barrier(jnp.mean(centered * centered, axis=-1, keepdims=True))
    inv_std = lax.rsqrt(variance + 1e-05)
    return (centered * inv_std, inv_std)

def reference(tokens, cell_mask, shifts, projection_in, projection_out, cotangent):
    scenes, grid_rows, col_count, model_dim = tokens.shape
    hidden_width = HEADS * HD
    shift_row = shifts[0].astype(jnp.int32)
    shift_col = shifts[1].astype(jnp.int32)
    score_scale = HD ** (-0.5)

    def rolled(grid_field):
        return roll_axis(roll_axis(grid_field, shift_row, 1), shift_col, 2)
    row_ids = (jnp.arange(grid_rows, dtype=jnp.int32) + shift_row) % grid_rows
    col_ids = (jnp.arange(col_count, dtype=jnp.int32) + shift_col) % col_count
    region = (row_ids < shift_row).astype(jnp.int32)[:, None] * 2 + (col_ids < shift_col).astype(jnp.int32)[None, :]
    region_all = jnp.broadcast_to(region[None, :, :, None], (scenes, grid_rows, col_count, 1))
    inputs = (group_windows(rolled(tokens)), group_windows(rolled(cell_mask)[..., None]), group_windows(region_all), group_windows(rolled(cotangent)))

    def block_step(carry, block):
        token_win, mask_win, region_win, cot_win = block
        window_count = token_win.shape[0]
        window_len = token_win.shape[1]
        region_ids = region_win[..., 0]
        mask_flag = mask_win[..., 0] > 0
        allowed = (region_ids[:, :, None] == region_ids[:, None, :]) & (mask_flag[:, None, :] | jnp.eye(window_len, dtype=bool)[None])
        normed, inv_std = normalize(token_win.astype(jnp.float32))
        normed_bf = normed.astype(jnp.bfloat16)
        flat_normed = normed_bf.reshape(-1, model_dim)
        packed_heads = jnp.dot(flat_normed, projection_in, preferred_element_type=jnp.float32).astype(jnp.bfloat16)
        packed_heads = packed_heads.reshape(window_count, window_len, 3, HEADS, HD)
        query_heads = packed_heads[:, :, 0].astype(jnp.float32)
        key_heads = packed_heads[:, :, 1].astype(jnp.float32)
        value_heads = packed_heads[:, :, 2].astype(jnp.float32)
        scores = jnp.einsum('wqhd,wkhd->whqk', query_heads, key_heads) * score_scale
        scores = jnp.where(allowed[:, None], scores, -1e+30)
        row_peak = lax.optimization_barrier(jnp.max(scores, axis=-1, keepdims=True))
        exp_terms = jnp.exp(scores - row_peak)
        attention = exp_terms / lax.optimization_barrier(jnp.sum(exp_terms, axis=-1, keepdims=True))
        attention_bf = attention.astype(jnp.bfloat16)
        context = jnp.einsum('whqk,wkhd->wqhd', attention_bf.astype(jnp.float32), value_heads).astype(jnp.bfloat16)
        flat_context = context.reshape(-1, hidden_width)
        projected = jnp.dot(flat_context, projection_out, preferred_element_type=jnp.float32)
        output_win = (token_win.astype(jnp.float32) + projected.reshape(token_win.shape)).astype(jnp.bfloat16)
        flat_cot = cot_win.reshape(-1, model_dim)
        grad_context = jnp.dot(flat_cot, projection_out.T, preferred_element_type=jnp.float32).astype(jnp.bfloat16)
        term_out = jnp.dot(flat_context.T, flat_cot, preferred_element_type=jnp.float32)
        grad_heads = grad_context.reshape(window_count, window_len, HEADS, HD).astype(jnp.float32)
        grad_attention = jnp.einsum('wqhd,wkhd->whqk', grad_heads, value_heads)
        grad_scores = (attention * (grad_attention - lax.optimization_barrier(jnp.sum(grad_attention * attention, axis=-1, keepdims=True))) * score_scale).astype(jnp.bfloat16)
        grad_scores_f = grad_scores.astype(jnp.float32)
        grad_query = jnp.einsum('whqk,wkhd->wqhd', grad_scores_f, key_heads)
        grad_key = jnp.einsum('whqk,wqhd->wkhd', grad_scores_f, query_heads)
        grad_value = jnp.einsum('whqk,wqhd->wkhd', attention_bf.astype(jnp.float32), grad_heads)
        grad_packed = jnp.stack([grad_query, grad_key, grad_value], axis=2).astype(jnp.bfloat16).reshape(-1, 3 * hidden_width)
        term_in = jnp.dot(flat_normed.T, grad_packed, preferred_element_type=jnp.float32)
        grad_normed = jnp.dot(grad_packed, projection_in.T, preferred_element_type=jnp.float32).reshape(token_win.shape)
        grad_win = (cot_win.astype(jnp.float32) + inv_std * (grad_normed - lax.optimization_barrier(jnp.mean(grad_normed, axis=-1, keepdims=True)) - normed * lax.optimization_barrier(jnp.mean(grad_normed * normed, axis=-1, keepdims=True)))).astype(jnp.bfloat16)
        return ((carry[0] + term_in, carry[1] + term_out), (output_win, grad_win))
    initial = (jnp.zeros((model_dim, 3 * hidden_width), jnp.float32), jnp.zeros((hidden_width, model_dim), jnp.float32))
    sums, stacked = lax.scan(block_step, initial, inputs)

    def restored(windowed):
        grid_field = ungroup_windows(windowed, scenes, grid_rows, col_count)
        return roll_axis(roll_axis(grid_field, grid_rows - shift_row, 1), col_count - shift_col, 2)
    return (restored(stacked[0]), restored(stacked[1]), sums[0], sums[1])
```

```python
import jax
import jax.numpy as jnp
import numpy as np
from jax import lax
from jax.sharding import PartitionSpec as P

HEADS = 8
HD = 64
WIN = 16


def stage_masks(rows):
    bits = [1 << b for b in range(rows.bit_length() - 1)]
    far = bits[:1:-1]
    return (far + bits[:2], far + bits[:2][::-1])


def slot_masks(rows, core):
    masks = [0]
    for m in stage_masks(rows)[core]:
        masks = masks + [a ^ m for a in masks]
    return np.array(masks, np.int32)


def exchange(block, rows, stage):
    masks = stage_masks(rows)
    pairs = [
        (c * rows + i, c * rows + (i ^ masks[c][stage])) for c in range(2) for i in range(rows)
    ]
    return lax.ppermute(block, ("fsdp", "rows"), pairs)


def swap_cores(block):
    return lax.ppermute(block, "fsdp", [(0, 1), (1, 0)])


def shifted(block, rows, distance):
    return lax.ppermute(block, "rows", [((i - distance) % rows, i) for i in range(rows)])


def slot_tables(rows):
    core = lax.axis_index("fsdp")
    me = lax.axis_index("rows")
    m0 = jnp.asarray(slot_masks(rows, 0))
    m1 = jnp.asarray(slot_masks(rows, 1))
    own = jnp.where(core == 0, m0, m1) ^ me
    other = jnp.where(core == 0, m1, m0) ^ me
    return core, own, other


def gather_rows(shard, rows, core, own, other):
    stages = len(stage_masks(rows)[0])
    held = shard[None]
    for stage in range(stages):
        held = jnp.concatenate([held, exchange(held, rows, stage)], axis=0)
    theirs = swap_cores(held)
    both = jnp.concatenate([held, theirs], axis=0)
    where = jnp.concatenate([core * rows + own, (1 - core) * rows + other])
    slot_of = jnp.argsort(where)
    return jnp.take(both, slot_of, axis=0).reshape(-1, shard.shape[-1])


def scatter_rows(term, rows, core, own, other):
    stages = len(stage_masks(rows)[0])
    blocks = term.reshape(2 * rows, -1, term.shape[-1])
    keep = jnp.take(blocks, core * rows + own, axis=0)
    send = jnp.take(blocks, (1 - core) * rows + other, axis=0).astype(jnp.bfloat16)
    keep = keep + swap_cores(send).astype(jnp.float32)
    for stage in range(stages - 1, -1, -1):
        half = keep.shape[0] // 2
        arrived = exchange(keep[half:].astype(jnp.bfloat16), rows, stage)
        keep = keep[:half] + arrived.astype(jnp.float32)
    return keep[0]


def body(tokens, cell_mask, shifts, projection_in, projection_out, cotangent):
    rows = lax.axis_size("rows")
    row_count, col_count, model_dim = tokens.shape[1:]
    cells = row_count * col_count
    hidden = HEADS * HD
    scale = HD ** (-0.5)
    s_row, s_col = shifts[0], shifts[1]
    core, own, other = slot_tables(rows)
    own_tokens = tokens.reshape(cells, model_dim)
    own_cot = cotangent.reshape(cells, model_dim)
    next_tokens = shifted(own_tokens, rows, -1)
    own_mask = cell_mask.astype(jnp.bfloat16).reshape(cells, 1)
    next_mask = shifted(own_mask, rows, -1)
    next_cot = shifted(own_cot, rows, -1)
    full_in = gather_rows(projection_in, rows, core, own, other)
    full_out = gather_rows(projection_out, rows, core, own, other)
    cell = jnp.arange(cells, dtype=jnp.int32)
    cell_row, cell_col = cell // col_count, cell % col_count
    borrowed = cell_row < s_row
    x = jnp.where(borrowed[:, None], next_tokens, own_tokens)
    cot = jnp.where(borrowed[:, None], next_cot, own_cot)
    key_ok = jnp.where(borrowed, next_mask[:, 0], own_mask[:, 0]) > 0
    last = lax.axis_index("rows") == rows - 1
    region = 2 * (borrowed & last).astype(jnp.int32) + (cell_col < s_col).astype(jnp.int32)
    allowed = (region[:, None] == region[None, :]) & (
        key_ok[None, :] | (cell[:, None] == cell[None, :])
    )
    xf = x.astype(jnp.float32)
    mean = jnp.mean(xf, axis=-1, keepdims=True)
    centered = xf - mean
    inv_std = lax.rsqrt(jnp.mean(centered * centered, axis=-1, keepdims=True) + 1e-05)
    normed = centered * inv_std
    normed_bf = normed.astype(jnp.bfloat16)
    packed = jnp.dot(normed_bf, full_in, preferred_element_type=jnp.float32).astype(jnp.bfloat16)
    packed = packed.reshape(cells, 3, HEADS, HD)
    q, k, v = packed[:, 0], packed[:, 1], packed[:, 2]
    f32 = jnp.float32
    scores = jnp.einsum("qhd,khd->hqk", q, k, preferred_element_type=f32) * scale
    scores = jnp.where(allowed[None], scores, -1e30)
    exp_terms = jnp.exp(scores - jnp.max(scores, axis=-1, keepdims=True))
    attention = exp_terms / jnp.sum(exp_terms, axis=-1, keepdims=True)
    attention_bf = attention.astype(jnp.bfloat16)
    context = jnp.einsum("hqk,khd->qhd", attention_bf, v, preferred_element_type=f32)
    context = context.astype(jnp.bfloat16).reshape(cells, hidden)
    own_context = jnp.where(borrowed[:, None], shifted(context, rows, 1), context)
    output = (
        own_tokens.astype(f32) + jnp.dot(own_context, full_out, preferred_element_type=f32)
    ).astype(jnp.bfloat16)
    grad_context = lax.dot_general(
        cot, full_out, (((1,), (1,)), ((), ())), preferred_element_type=f32
    ).astype(jnp.bfloat16)
    term_out = lax.dot_general(context, cot, (((0,), (0,)), ((), ())), preferred_element_type=f32)
    grad_out = scatter_rows(term_out, rows, core, own, other)
    gh = grad_context.reshape(cells, HEADS, HD)
    grad_attention = jnp.einsum("qhd,khd->hqk", gh, v, preferred_element_type=f32)
    grad_scores = (
        attention
        * (grad_attention - jnp.sum(grad_attention * attention, axis=-1, keepdims=True))
        * scale
    ).astype(jnp.bfloat16)
    gq = jnp.einsum("hqk,khd->qhd", grad_scores, k, preferred_element_type=f32)
    gk = jnp.einsum("hqk,qhd->khd", grad_scores, q, preferred_element_type=f32)
    gv = jnp.einsum("hqk,qhd->khd", attention_bf, gh, preferred_element_type=f32)
    gp = jnp.stack([gq, gk, gv], axis=1).astype(jnp.bfloat16).reshape(cells, 3 * hidden)
    term_in = lax.dot_general(normed_bf, gp, (((0,), (0,)), ((), ())), preferred_element_type=f32)
    grad_in = scatter_rows(term_in, rows, core, own, other)
    gn = lax.dot_general(gp, full_in, (((1,), (1,)), ((), ())), preferred_element_type=f32)
    grad_win = (
        cot.astype(f32)
        + inv_std
        * (
            gn
            - jnp.mean(gn, axis=-1, keepdims=True)
            - normed * jnp.mean(gn * normed, axis=-1, keepdims=True)
        )
    ).astype(jnp.bfloat16)
    own_grad = jnp.where(borrowed[:, None], shifted(grad_win, rows, 1), grad_win)
    shape = tokens.shape
    return (output.reshape(shape), own_grad.reshape(shape), grad_in, grad_out)


def solution(mesh):
    placed = (
        P(("groups", "fsdp"), "rows", None, None),
        P(("groups", "fsdp"), "rows", None),
        P(),
        P(("fsdp", "rows"), None),
        P(("fsdp", "rows"), None),
        P(("groups", "fsdp"), "rows", None, None),
    )
    return jax.shard_map(
        body,
        mesh=mesh,
        in_specs=placed,
        out_specs=(
            P(("groups", "fsdp"), "rows", None, None),
            P(("groups", "fsdp"), "rows", None, None),
            P(("groups", "fsdp", "rows"), None),
            P(("groups", "fsdp", "rows"), None),
        ),
        check_vma=False,
    )
```

```python
import functools

import jax
import jax.numpy as jnp
import numpy as np
from jax import lax
from jax.experimental import pallas as pl
from jax.experimental.pallas import tpu as pltpu
from jax.sharding import PartitionSpec as P

HEADS = 8
HD = 64
PAIR = 2 * HD
F32 = jnp.float32
BF16 = jnp.bfloat16
VM = pl.BlockSpec(memory_space=pltpu.VMEM)
SM = pl.BlockSpec(memory_space=pltpu.SMEM)


def stage_masks(rows):
    bits = [1 << b for b in range(rows.bit_length() - 1)]
    far = bits[:1:-1]
    return (far + bits[:2], far + bits[:2][::-1])


def slot_masks(rows, core):
    masks = [0]
    for m in stage_masks(rows)[core]:
        masks = masks + [a ^ m for a in masks]
    return np.array(masks, np.int32)


def exchange(block, rows, stage):
    masks = stage_masks(rows)
    pairs = [
        (c * rows + i, c * rows + (i ^ masks[c][stage])) for c in range(2) for i in range(rows)
    ]
    return lax.ppermute(block, ("fsdp", "rows"), pairs)


def swap_cores(block):
    return lax.ppermute(block, "fsdp", [(0, 1), (1, 0)])


def shifted(block, rows, distance):
    return lax.ppermute(block, "rows", [((i - distance) % rows, i) for i in range(rows)])


def call(kernel, outs, specs, scratch=(), flops=0, moved=0, name=None):
    return pl.pallas_call(
        kernel,
        out_shape=tuple(jax.ShapeDtypeStruct(s, d) for s, d in outs),
        in_specs=list(specs),
        out_specs=tuple(VM for _ in outs),
        scratch_shapes=list(scratch),
        compiler_params=pltpu.CompilerParams(vmem_limit_bytes=40 << 20),
        cost_estimate=pl.CostEstimate(flops=flops, bytes_accessed=moved, transcendentals=0),
        name=name,
    )


def dot(a, b, ca=1, cb=0):
    return lax.dot_general(a, b, (((ca,), (cb,)), ((), ())), preferred_element_type=F32)


def place(dst, src, table, first, count, size):
    def step(j, carry):
        at = pl.multiple_of(table[first + j] * size, size)
        dst[pl.ds(at, size), :] = src[pl.ds(pl.multiple_of(j * size, size), size), :]
        return carry

    lax.fori_loop(0, count, step, 0)


def pick(dst, src, table, count, size):
    def step(j, carry):
        at = pl.multiple_of(table[j] * size, size)
        dst[pl.ds(pl.multiple_of(j * size, size), size), :] = src[pl.ds(at, size), :]
        return carry

    lax.fori_loop(0, count, step, 0)


def borrowed_rows(scal, low, count, cols, forward):
    row = (lax.broadcasted_iota(jnp.int32, (count, 1), 0) + low) // cols
    return row < scal[0] if forward else row >= scal[0]


def norm_kernel(scal, table, own, halo, xw, normed_bf, ordered, mean_out, inv_out, turned, *, low, cols, forward, blocks):
    half = halo.shape[0]
    take = borrowed_rows(scal, low, half, cols, forward)
    keep_low = half - low
    xw[pl.ds(keep_low, half), :] = own[pl.ds(keep_low, half), :]
    mixed = jnp.where(take, halo[...].astype(F32), own[pl.ds(low, half), :].astype(F32))
    xw[pl.ds(low, half), :] = mixed.astype(BF16)
    x = xw[...].astype(F32)
    mean = jnp.mean(x, axis=-1, keepdims=True)
    centered = x - mean
    inv = lax.rsqrt(jnp.mean(centered * centered, axis=-1, keepdims=True) + 1e-05)
    normed = centered * inv
    normed_bf[...] = normed.astype(BF16)
    mean_out[...] = mean
    inv_out[...] = inv
    turned[...] = normed.T.astype(BF16)
    pick(ordered, turned, table, blocks, turned.shape[0] // blocks)


def forward_kernel(place_at, order, normed_bf, bias, w0, w1, w2, w3, full, packed, attn, ctx, ctx_ordered, turned, *, blocks):
    size = full.shape[0] // blocks
    quarter = blocks // 4
    for i, w in enumerate((w0, w1, w2, w3)):
        place(full, w, place_at, i * quarter, quarter, size)
    hidden = ctx.shape[1]
    packed[...] = dot(normed_bf[...], full[...]).astype(BF16)
    cells = normed_bf.shape[0]
    first = lax.broadcasted_iota(jnp.int32, (cells, PAIR), 1) < HD
    for p in range(HEADS // 2):
        lanes = pl.ds(p * PAIR, PAIR)
        q = packed[:, lanes].astype(F32)
        k = packed[:, pl.ds(hidden + p * PAIR, PAIR)]
        v = packed[:, pl.ds(2 * hidden + p * PAIR, PAIR)]
        parts = []
        for side in range(2):
            q_one = jnp.where(first if side == 0 else ~first, q, 0.0).astype(BF16)
            scores = dot(q_one, k, 1, 1) * (HD ** (-0.5)) + bias[...]
            e = jnp.exp(scores - jnp.max(scores, axis=-1, keepdims=True))
            a = e * (1.0 / jnp.sum(e, axis=-1, keepdims=True))
            attn[2 * p + side] = a
            parts.append(dot(a.astype(BF16), v))
        both = jnp.where(first, parts[0], parts[1])
        ctx[:, lanes] = both.astype(BF16)
        turned[lanes, :] = both.T.astype(BF16)
    pick(ctx_ordered, turned, order, blocks, turned.shape[0] // blocks)


def term_out_kernel(scal, ctx_ordered, own, halo, cot, keep, send, *, low, cols, forward):
    half = halo.shape[0]
    take = borrowed_rows(scal, low, half, cols, forward)
    keep_low = half - low
    cot[pl.ds(keep_low, half), :] = own[pl.ds(keep_low, half), :]
    cot[pl.ds(low, half), :] = jnp.where(
        take, halo[...].astype(F32), own[pl.ds(low, half), :].astype(F32)
    ).astype(BF16)
    n = keep.shape[0]
    send[...] = dot(ctx_ordered[pl.ds(n, n), :], cot[...]).astype(BF16)
    keep[...] = dot(ctx_ordered[pl.ds(0, n), :], cot[...])


def backward_kernel(place_at, cot, packed, attn, ordered, w0, w1, w2, w3, full, gp, keep, send, gctx, *, blocks):
    size = full.shape[0] // blocks
    quarter = blocks // 4
    for i, w in enumerate((w0, w1, w2, w3)):
        place(full, w, place_at, i * quarter, quarter, size)
    hidden = full.shape[0]
    cells = cot.shape[0]
    gctx[...] = dot(cot[...], full[...], 1, 1).astype(BF16)
    first = lax.broadcasted_iota(jnp.int32, (cells, PAIR), 1) < HD
    for p in range(HEADS // 2):
        lanes = pl.ds(p * PAIR, PAIR)
        q = packed[:, lanes]
        k = packed[:, pl.ds(hidden + p * PAIR, PAIR)]
        v = packed[:, pl.ds(2 * hidden + p * PAIR, PAIR)]
        g = gctx[:, lanes]
        gf = g.astype(F32)
        gq, gk, gv = [], [], []
        for side in range(2):
            g_one = jnp.where(first if side == 0 else ~first, gf, 0.0).astype(BF16)
            a = attn[2 * p + side]
            ga = dot(g_one, v, 1, 1)
            inner = jnp.sum(ga * a, axis=-1, keepdims=True)
            gs = (a * (ga - inner) * (HD ** (-0.5))).astype(BF16)
            gq.append(dot(gs, k))
            gk.append(dot(gs, q, 0, 0))
            gv.append(dot(a.astype(BF16), g, 0, 0))
        gp[:, lanes] = jnp.where(first, gq[0], gq[1]).astype(BF16)
        gp[:, pl.ds(hidden + p * PAIR, PAIR)] = jnp.where(first, gk[0], gk[1]).astype(BF16)
        gp[:, pl.ds(2 * hidden + p * PAIR, PAIR)] = jnp.where(first, gv[0], gv[1]).astype(BF16)
    n = keep.shape[0]
    send[...] = dot(ordered[pl.ds(n, n), :], gp[...]).astype(BF16)
    keep[...] = dot(ordered[pl.ds(0, n), :], gp[...])


def grad_kernel(xw, mean, inv, gp, full, cot, grad):
    gn = dot(gp[...], full[...], 1, 1)
    normed = (xw[...].astype(F32) - mean[...]) * inv[...]
    m1 = jnp.mean(gn, axis=-1, keepdims=True)
    m2 = jnp.mean(gn * normed, axis=-1, keepdims=True)
    grad[...] = (cot[...].astype(F32) + inv[...] * (gn - m1 - normed * m2)).astype(BF16)


def output_kernel(scal, own, ctx, back, full, out, mixed, *, low, cols, forward):
    half = back.shape[0]
    take = borrowed_rows(scal, low, half, cols, forward)
    keep_low = half - low
    mixed[pl.ds(keep_low, half), :] = ctx[pl.ds(keep_low, half), :]
    mixed[pl.ds(low, half), :] = jnp.where(
        take, back[...].astype(F32), ctx[pl.ds(low, half), :].astype(F32)
    ).astype(BF16)
    out[...] = (own[...].astype(F32) + dot(mixed[...], full[...])).astype(BF16)


def gather_parts(shard, rows):
    stages = len(stage_masks(rows)[0])
    held = shard
    for stage in range(stages - 1):
        held = jnp.concatenate([held, exchange(held, rows, stage)], axis=0)
    last = exchange(held, rows, stages - 1)
    return held, last, swap_cores(held), swap_cores(last)


def scatter_parts(keep, send, rows):
    stages = len(stage_masks(rows)[0])
    keep = keep + swap_cores(send).astype(F32)
    for stage in range(stages - 1, -1, -1):
        half = keep.shape[0] // 2
        arrived = exchange(keep[half:].astype(BF16), rows, stage)
        keep = keep[:half] + arrived.astype(F32)
    return keep


def branch(tokens, cell_mask, shifts, projection_in, projection_out, cotangent, *, forward):
    rows = lax.axis_size("rows")
    row_count, cols, dim = tokens.shape[1:]
    cells = row_count * cols
    half = cells // 2
    hidden = HEADS * HD
    low = 0 if forward else half
    distance = -1 if forward else 1
    core = lax.axis_index("fsdp")
    me = lax.axis_index("rows")
    blocks = 2 * rows
    m0 = jnp.asarray(slot_masks(rows, 0))
    m1 = jnp.asarray(slot_masks(rows, 1))
    mine = jnp.where(core == 0, m0, m1) ^ me
    theirs = jnp.where(core == 0, m1, m0) ^ me
    table = jnp.concatenate([core * rows + mine, (1 - core) * rows + theirs]).astype(jnp.int32)
    scal = shifts.astype(jnp.int32)
    s_row, s_col = scal[0], scal[1]
    part = lambda a: lax.slice_in_dim(a, low, low + half, axis=0)

    own = tokens.reshape(cells, dim)
    own_cot = cotangent.reshape(cells, dim)
    own_mask = cell_mask.astype(BF16).reshape(cells, 1)
    halo = shifted(part(own), rows, distance)
    halo_mask = shifted(part(own_mask), rows, distance)
    in_parts = gather_parts(projection_in, rows)
    out_parts = gather_parts(projection_out, rows)
    halo_cot = shifted(part(own_cot), rows, distance)

    cell = jnp.arange(cells, dtype=jnp.int32)
    cell_row, cell_col = cell // cols, cell % cols
    from_other = (cell_row < s_row) if forward else (cell_row >= s_row)
    pad = ((low, half - low), (0, 0))
    key_ok = jnp.where(from_other, jnp.pad(halo_mask, pad)[:, 0], own_mask[:, 0]) > 0
    at_wrap = me == (rows - 1 if forward else 0)
    region = 2 * ((cell_row < s_row) & at_wrap).astype(jnp.int32) + (cell_col < s_col).astype(
        jnp.int32
    )
    allowed = (region[:, None] == region[None, :]) & (
        key_ok[None, :] | (cell[:, None] == cell[None, :])
    )
    bias = jnp.where(allowed, 0.0, -1e30).astype(F32)

    shape_kw = dict(low=low, cols=cols, forward=forward)
    xw, normed_bf, ordered, mean, inv = call(
        functools.partial(norm_kernel, blocks=blocks, **shape_kw),
        [((cells, dim), BF16), ((cells, dim), BF16), ((dim, cells), BF16), ((cells, 1), F32), ((cells, 1), F32)],
        [SM, SM, VM, VM],
        [pltpu.VMEM((dim, cells), BF16)],
        flops=20 * cells * dim,
        moved=10 * cells * dim,
        name="norm",
    )(scal, table, own, halo)
    full_in, packed, attn, ctx, ctx_ordered = call(
        functools.partial(forward_kernel, blocks=blocks),
        [((dim, 3 * hidden), BF16), ((cells, 3 * hidden), BF16), ((HEADS, cells, cells), F32), ((cells, hidden), BF16), ((hidden, cells), BF16)],
        [SM, SM, VM, VM, VM, VM, VM, VM],
        [pltpu.VMEM((hidden, cells), BF16)],
        flops=6 * cells * dim * 3 * hidden,
        moved=10 << 20,
        name="fwd",
    )(table, table, normed_bf, bias, *in_parts)
    back_ctx = shifted(part(ctx), rows, -distance)
    cot, keep_out, send_out = call(
        functools.partial(term_out_kernel, **shape_kw),
        [((cells, dim), BF16), ((hidden // 2, dim), F32), ((hidden // 2, dim), BF16)],
        [SM, VM, VM, VM],
        flops=2 * cells * dim * hidden,
        moved=4 << 20,
        name="term_out",
    )(scal, ctx_ordered, own_cot, halo_cot)
    grad_out = scatter_parts(keep_out, send_out, rows)
    full_out, gp, keep_in, send_in = call(
        functools.partial(backward_kernel, blocks=blocks),
        [((hidden, dim), BF16), ((cells, 3 * hidden), BF16), ((dim // 2, 3 * hidden), F32), ((dim // 2, 3 * hidden), BF16)],
        [SM, VM, VM, VM, VM, VM, VM, VM, VM],
        [pltpu.VMEM((cells, hidden), BF16)],
        flops=8 * cells * dim * 3 * hidden,
        moved=12 << 20,
        name="bwd",
    )(table, cot, packed, attn, ordered, *out_parts)
    grad_in = scatter_parts(keep_in, send_in, rows)
    (grad_win,) = call(
        grad_kernel,
        [((cells, dim), BF16)],
        [VM] * 6,
        flops=2 * cells * dim * 3 * hidden,
        moved=6 << 20,
        name="grad",
    )(xw, mean, inv, gp, full_in, cot)
    back_grad = shifted(part(grad_win), rows, -distance)
    (output,) = call(
        functools.partial(output_kernel, **shape_kw),
        [((cells, dim), BF16)],
        [SM, VM, VM, VM, VM],
        [pltpu.VMEM((cells, hidden), BF16)],
        flops=2 * cells * dim * hidden,
        moved=3 << 20,
        name="output",
    )(scal, own, ctx, back_ctx, full_out)
    own_grad = jnp.where(from_other[:, None], jnp.pad(back_grad, pad), grad_win)
    shape = tokens.shape
    return (output.reshape(shape), own_grad.reshape(shape), grad_in, grad_out)


def body(tokens, cell_mask, shifts, projection_in, projection_out, cotangent):
    return lax.cond(
        shifts[0] <= tokens.shape[1] // 2,
        functools.partial(branch, forward=True),
        functools.partial(branch, forward=False),
        tokens, cell_mask, shifts, projection_in, projection_out, cotangent,
    )


def solution(mesh):
    placed = (
        P(("groups", "fsdp"), "rows", None, None),
        P(("groups", "fsdp"), "rows", None),
        P(),
        P(("fsdp", "rows"), None),
        P(("fsdp", "rows"), None),
        P(("groups", "fsdp"), "rows", None, None),
    )
    return jax.shard_map(
        body,
        mesh=mesh,
        in_specs=placed,
        out_specs=(
            P(("groups", "fsdp"), "rows", None, None),
            P(("groups", "fsdp"), "rows", None, None),
            P(("groups", "fsdp", "rows"), None),
            P(("groups", "fsdp", "rows"), None),
        ),
        check_vma=False,
    )
```

```python
import functools

import jax
import jax.numpy as jnp
import numpy as np
from jax import lax
from jax.experimental import pallas as pl
from jax.experimental.pallas import tpu as pltpu
from jax.sharding import PartitionSpec as P

HEADS = 8
HD = 64
PAIR = 2 * HD
F32 = jnp.float32
BF16 = jnp.bfloat16
VM = pl.BlockSpec(memory_space=pltpu.VMEM)
SM = pl.BlockSpec(memory_space=pltpu.SMEM)


def stage_masks(rows):
    bits = [1 << b for b in range(rows.bit_length() - 1)]
    far = bits[:1:-1]
    return (far + bits[:2], far + bits[:2][::-1])


def slot_masks(rows, core):
    masks = [0]
    for m in stage_masks(rows)[core]:
        masks = masks + [a ^ m for a in masks]
    return np.array(masks, np.int32)


def exchange(block, rows, stage):
    masks = stage_masks(rows)
    pairs = [
        (c * rows + i, c * rows + (i ^ masks[c][stage])) for c in range(2) for i in range(rows)
    ]
    return lax.ppermute(block, ("fsdp", "rows"), pairs)


def swap_cores(block):
    return lax.ppermute(block, "fsdp", [(0, 1), (1, 0)])


def shifted(block, rows, distance):
    return lax.ppermute(block, "rows", [((i - distance) % rows, i) for i in range(rows)])


def call(kernel, outs, specs, scratch=(), flops=0, moved=0, name=None):
    return pl.pallas_call(
        kernel,
        out_shape=tuple(jax.ShapeDtypeStruct(s, d) for s, d in outs),
        in_specs=list(specs),
        out_specs=tuple(VM for _ in outs),
        scratch_shapes=list(scratch),
        compiler_params=pltpu.CompilerParams(vmem_limit_bytes=40 << 20),
        cost_estimate=pl.CostEstimate(flops=flops, bytes_accessed=moved, transcendentals=0),
        name=name,
    )


def dot(a, b, ca=1, cb=0):
    return lax.dot_general(a, b, (((ca,), (cb,)), ((), ())), preferred_element_type=F32)


def place(dst, src, table, first, count, size):
    def step(j, carry):
        at = pl.multiple_of(table[first + j] * size, size)
        dst[pl.ds(at, size), :] = src[pl.ds(pl.multiple_of(j * size, size), size), :]
        return carry

    lax.fori_loop(0, count, step, 0)


def pick(dst, src, table, count, size):
    def step(j, carry):
        at = pl.multiple_of(table[j] * size, size)
        dst[pl.ds(pl.multiple_of(j * size, size), size), :] = src[pl.ds(at, size), :]
        return carry

    lax.fori_loop(0, count, step, 0)


def borrowed_rows(scal, low, count, cols, forward):
    row = (lax.broadcasted_iota(jnp.int32, (count, 1), 0) + low) // cols
    return row < scal[0] if forward else row >= scal[0]


def norm_kernel(scal, table, own, halo, xw, normed_bf, ordered, mean_out, inv_out, turned, *, low, cols, forward, blocks):
    half = halo.shape[0]
    take = borrowed_rows(scal, low, half, cols, forward)
    keep_low = half - low
    xw[pl.ds(keep_low, half), :] = own[pl.ds(keep_low, half), :]
    mixed = jnp.where(take, halo[...].astype(F32), own[pl.ds(low, half), :].astype(F32))
    xw[pl.ds(low, half), :] = mixed.astype(BF16)
    x = xw[...].astype(F32)
    mean = jnp.mean(x, axis=-1, keepdims=True)
    centered = x - mean
    inv = lax.rsqrt(jnp.mean(centered * centered, axis=-1, keepdims=True) + 1e-05)
    normed = centered * inv
    normed_bf[...] = normed.astype(BF16)
    mean_out[...] = mean
    inv_out[...] = inv
    turned[...] = normed.T.astype(BF16)
    pick(ordered, turned, table, blocks, turned.shape[0] // blocks)


def forward_kernel(place_at, order, normed_bf, bias, w0, w1, w2, w3, full, packed, attn, ctx, ctx_ordered, turned, *, blocks):
    size = full.shape[0] // blocks
    quarter = blocks // 4
    for i, w in enumerate((w0, w1, w2, w3)):
        place(full, w, place_at, i * quarter, quarter, size)
    hidden = ctx.shape[1]
    packed[...] = dot(normed_bf[...], full[...]).astype(BF16)
    cells = normed_bf.shape[0]
    first = lax.broadcasted_iota(jnp.int32, (cells, PAIR), 1) < HD
    for p in range(HEADS // 2):
        lanes = pl.ds(p * PAIR, PAIR)
        q = packed[:, lanes].astype(F32)
        k = packed[:, pl.ds(hidden + p * PAIR, PAIR)]
        v = packed[:, pl.ds(2 * hidden + p * PAIR, PAIR)]
        parts = []
        for side in range(2):
            q_one = jnp.where(first if side == 0 else ~first, q, 0.0).astype(BF16)
            scores = dot(q_one, k, 1, 1) * (HD ** (-0.5)) + bias[...]
            e = jnp.exp(scores - jnp.max(scores, axis=-1, keepdims=True))
            a = e * (1.0 / jnp.sum(e, axis=-1, keepdims=True))
            attn[2 * p + side] = a
            parts.append(dot(a.astype(BF16), v))
        both = jnp.where(first, parts[0], parts[1])
        ctx[:, lanes] = both.astype(BF16)
        turned[lanes, :] = both.T.astype(BF16)
    pick(ctx_ordered, turned, order, blocks, turned.shape[0] // blocks)


def term_out_kernel(scal, ctx_ordered, own, halo, cot, keep, send, *, low, cols, forward):
    half = halo.shape[0]
    take = borrowed_rows(scal, low, half, cols, forward)
    keep_low = half - low
    cot[pl.ds(keep_low, half), :] = own[pl.ds(keep_low, half), :]
    cot[pl.ds(low, half), :] = jnp.where(
        take, halo[...].astype(F32), own[pl.ds(low, half), :].astype(F32)
    ).astype(BF16)
    n = keep.shape[0]
    send[...] = dot(ctx_ordered[pl.ds(n, n), :], cot[...]).astype(BF16)
    keep[...] = dot(ctx_ordered[pl.ds(0, n), :], cot[...])


def half_backward(packed, attn, gctx, gp, first_pair, pairs):
    cells = packed.shape[0]
    hidden = packed.shape[1] // 3
    width = pairs * PAIR
    first = lax.broadcasted_iota(jnp.int32, (cells, PAIR), 1) < HD
    for i in range(pairs):
        p = first_pair + i
        q = packed[:, pl.ds(p * PAIR, PAIR)]
        k = packed[:, pl.ds(hidden + p * PAIR, PAIR)]
        v = packed[:, pl.ds(2 * hidden + p * PAIR, PAIR)]
        g = gctx[:, pl.ds(p * PAIR, PAIR)]
        gf = g.astype(F32)
        gq, gk, gv = [], [], []
        for side in range(2):
            g_one = jnp.where(first if side == 0 else ~first, gf, 0.0).astype(BF16)
            a = attn[2 * p + side]
            ga = dot(g_one, v, 1, 1)
            inner = jnp.sum(ga * a, axis=-1, keepdims=True)
            gs = (a * (ga - inner) * (HD ** (-0.5))).astype(BF16)
            gq.append(dot(gs, k))
            gk.append(dot(gs, q, 0, 0))
            gv.append(dot(a.astype(BF16), g, 0, 0))
        for t, two in enumerate((gq, gk, gv)):
            gp[:, pl.ds(t * width + i * PAIR, PAIR)] = jnp.where(first, two[0], two[1]).astype(BF16)


def term_of(ordered, gp, keep, send):
    n = keep.shape[0]
    send[...] = dot(ordered[pl.ds(n, n), :], gp[...]).astype(BF16)
    keep[...] = dot(ordered[pl.ds(0, n), :], gp[...])


def backward_a_kernel(place_at, cot, packed, attn, ordered, w0, w1, w2, w3, full, gctx, gp, keep, send, *, blocks):
    size = full.shape[0] // blocks
    quarter = blocks // 4
    for i, w in enumerate((w0, w1, w2, w3)):
        place(full, w, place_at, i * quarter, quarter, size)
    gctx[...] = dot(cot[...], full[...], 1, 1).astype(BF16)
    half_backward(packed, attn, gctx, gp, 0, HEADS // 4)
    term_of(ordered, gp, keep, send)


def backward_b_kernel(packed, attn, gctx, ordered, gp, keep, send):
    half_backward(packed, attn, gctx, gp, HEADS // 4, HEADS // 4)
    term_of(ordered, gp, keep, send)


def grad_kernel(xw, mean, inv, gp_a, gp_b, full, cot, grad, gp):
    width = gp.shape[1] // 6
    for t in range(3):
        gp[:, pl.ds(2 * t * width, width)] = gp_a[:, pl.ds(t * width, width)]
        gp[:, pl.ds((2 * t + 1) * width, width)] = gp_b[:, pl.ds(t * width, width)]
    gn = dot(gp[...], full[...], 1, 1)
    normed = (xw[...].astype(F32) - mean[...]) * inv[...]
    m1 = jnp.mean(gn, axis=-1, keepdims=True)
    m2 = jnp.mean(gn * normed, axis=-1, keepdims=True)
    grad[...] = (cot[...].astype(F32) + inv[...] * (gn - m1 - normed * m2)).astype(BF16)


def output_kernel(scal, own, ctx, back, full, out, mixed, *, low, cols, forward):
    half = back.shape[0]
    take = borrowed_rows(scal, low, half, cols, forward)
    keep_low = half - low
    mixed[pl.ds(keep_low, half), :] = ctx[pl.ds(keep_low, half), :]
    mixed[pl.ds(low, half), :] = jnp.where(
        take, back[...].astype(F32), ctx[pl.ds(low, half), :].astype(F32)
    ).astype(BF16)
    out[...] = (own[...].astype(F32) + dot(mixed[...], full[...])).astype(BF16)


def after(value, *done):
    return lax.optimization_barrier((value, *done))[0]


def gather_parts(shard, rows, waits):
    stages = len(stage_masks(rows)[0])
    held, arrived = shard, []
    for stage in range(stages - 1):
        got = exchange(after(held, *waits[stage]) if waits[stage] else held, rows, stage)
        arrived.append(got)
        held = jnp.concatenate([held, got], axis=0)
    last = exchange(after(held, *waits[-1]) if waits[-1] else held, rows, stages - 1)
    arrived.append(last)
    return (held, last, swap_cores(held), swap_cores(last)), arrived


def scatter_from(keep, arrived, rows):
    stages = len(stage_masks(rows)[0])
    keep = keep + arrived.astype(F32)
    first, seen = keep, []
    for stage in range(stages - 1, -1, -1):
        half = keep.shape[0] // 2
        arrived = exchange(keep[half:].astype(BF16), rows, stage)
        seen.append(arrived)
        if stage:
            keep = keep[:half] + arrived.astype(F32)
    return keep[: keep.shape[0] // 2], arrived, first, seen


def finish_kernel(keep_a, last_a, keep_b, last_b, out):
    fine = keep_a.shape[1] // 3
    for i, (keep, last) in enumerate(((keep_a, last_a), (keep_b, last_b))):
        for t in range(3):
            cols = pl.ds(t * fine, fine)
            out[:, pl.ds((2 * t + i) * fine, fine)] = keep[:, cols] + last[:, cols].astype(F32)


def branch(tokens, cell_mask, shifts, projection_in, projection_out, cotangent, *, forward):
    rows = lax.axis_size("rows")
    row_count, cols, dim = tokens.shape[1:]
    cells = row_count * cols
    half = cells // 2
    hidden = HEADS * HD
    low = 0 if forward else half
    distance = -1 if forward else 1
    core = lax.axis_index("fsdp")
    me = lax.axis_index("rows")
    blocks = 2 * rows
    m0 = jnp.asarray(slot_masks(rows, 0))
    m1 = jnp.asarray(slot_masks(rows, 1))
    mine = jnp.where(core == 0, m0, m1) ^ me
    theirs = jnp.where(core == 0, m1, m0) ^ me
    table = jnp.concatenate([core * rows + mine, (1 - core) * rows + theirs]).astype(jnp.int32)
    scal = shifts.astype(jnp.int32)
    s_row, s_col = scal[0], scal[1]
    part = lambda a: lax.slice_in_dim(a, low, low + half, axis=0)

    own = tokens.reshape(cells, dim)
    own_cot = cotangent.reshape(cells, dim)
    own_mask = cell_mask.astype(BF16).reshape(cells, 1)
    halo = shifted(part(own), rows, distance)
    halo_mask = shifted(part(own_mask), rows, distance)
    stages = len(stage_masks(rows)[0])
    waits = [()] * stages
    waits[1] = (halo, halo_mask)
    in_parts, in_got = gather_parts(projection_in, rows, waits)
    waits = [(in_got[t],) for t in range(stages)]
    out_parts, out_got = gather_parts(projection_out, rows, waits)
    halo_cot = shifted(after(part(own_cot), in_got[-1]), rows, distance)

    cell = jnp.arange(cells, dtype=jnp.int32)
    cell_row, cell_col = cell // cols, cell % cols
    from_other = (cell_row < s_row) if forward else (cell_row >= s_row)
    pad = ((low, half - low), (0, 0))
    key_ok = jnp.where(from_other, jnp.pad(halo_mask, pad)[:, 0], own_mask[:, 0]) > 0
    at_wrap = me == (rows - 1 if forward else 0)
    region = 2 * ((cell_row < s_row) & at_wrap).astype(jnp.int32) + (cell_col < s_col).astype(
        jnp.int32
    )
    allowed = (region[:, None] == region[None, :]) & (
        key_ok[None, :] | (cell[:, None] == cell[None, :])
    )
    bias = jnp.where(allowed, 0.0, -1e30).astype(F32)

    shape_kw = dict(low=low, cols=cols, forward=forward)
    xw, normed_bf, ordered, mean, inv = call(
        functools.partial(norm_kernel, blocks=blocks, **shape_kw),
        [((cells, dim), BF16), ((cells, dim), BF16), ((dim, cells), BF16), ((cells, 1), F32), ((cells, 1), F32)],
        [SM, SM, VM, VM],
        [pltpu.VMEM((dim, cells), BF16)],
        flops=20 * cells * dim,
        moved=10 * cells * dim,
        name="norm",
    )(scal, table, own, halo)
    full_in, packed, attn, ctx, ctx_ordered = call(
        functools.partial(forward_kernel, blocks=blocks),
        [((dim, 3 * hidden), BF16), ((cells, 3 * hidden), BF16), ((HEADS, cells, cells), F32), ((cells, hidden), BF16), ((hidden, cells), BF16)],
        [SM, SM, VM, VM, VM, VM, VM, VM],
        [pltpu.VMEM((hidden, cells), BF16)],
        flops=6 * cells * dim * 3 * hidden,
        moved=10 << 20,
        name="fwd",
    )(table, table, normed_bf, bias, *in_parts)
    back_ctx = shifted(part(ctx), rows, -distance)
    cot, keep_out, send_out = call(
        functools.partial(term_out_kernel, **shape_kw),
        [((cells, dim), BF16), ((hidden // 2, dim), F32), ((hidden // 2, dim), BF16)],
        [SM, VM, VM, VM],
        flops=2 * cells * dim * hidden,
        moved=4 << 20,
        name="term_out",
    )(scal, ctx_ordered, own_cot, halo_cot)
    swapped_out = swap_cores(send_out)
    quart = 3 * hidden // 2
    half_outs = [((cells, quart), BF16), ((dim // 2, quart), F32), ((dim // 2, quart), BF16)]
    full_out, gctx, gp_a, keep_a, send_a = call(
        functools.partial(backward_a_kernel, blocks=blocks),
        [((hidden, dim), BF16), ((cells, hidden), BF16)] + half_outs,
        [SM, VM, VM, VM, VM, VM, VM, VM, VM],
        flops=4 * cells * dim * 3 * hidden,
        moved=6 << 20,
        name="bwd_a",
    )(table, cot, packed, attn, ordered, *out_parts)
    swapped_a = swap_cores(send_a)
    gp_b, keep_b, send_b = call(
        backward_b_kernel,
        half_outs,
        [VM, VM, VM, VM],
        flops=4 * cells * dim * 3 * hidden,
        moved=6 << 20,
        name="bwd_b",
    )(packed, attn, after(gctx, swapped_out), ordered)
    swapped_b = swap_cores(send_b)
    kept_out, last_out, _, _ = scatter_from(keep_out, swapped_out, rows)
    grad_out = kept_out + last_out.astype(F32)
    kept_a, last_a, first_a, seen_a = scatter_from(keep_a, swapped_a, rows)
    kept_b, last_b, _, _ = scatter_from(keep_b, swapped_b, rows)
    (grad_in,) = call(
        finish_kernel,
        [((dim // blocks, 3 * hidden), F32)],
        [VM] * 4,
        moved=1 << 20,
        name="finish",
    )(kept_a, last_a, kept_b, last_b)
    (grad_win,) = call(
        grad_kernel,
        [((cells, dim), BF16)],
        [VM] * 7,
        [pltpu.VMEM((cells, 3 * hidden), BF16)],
        flops=2 * cells * dim * 3 * hidden,
        moved=6 << 20,
        name="grad",
    )(xw, mean, inv, gp_a, after(gp_b, back_ctx, first_a), full_in, cot)
    back_grad = shifted(part(grad_win), rows, -distance)
    (output,) = call(
        functools.partial(output_kernel, **shape_kw),
        [((cells, dim), BF16)],
        [SM, VM, VM, VM, VM],
        [pltpu.VMEM((cells, hidden), BF16)],
        flops=2 * cells * dim * hidden,
        moved=3 << 20,
        name="output",
    )(scal, own, ctx, after(back_ctx, seen_a[0]), full_out)
    own_grad = jnp.where(from_other[:, None], jnp.pad(back_grad, pad), grad_win)
    shape = tokens.shape
    return (output.reshape(shape), own_grad.reshape(shape), grad_in, grad_out)


def body(tokens, cell_mask, shifts, projection_in, projection_out, cotangent):
    return lax.cond(
        shifts[0] <= tokens.shape[1] // 2,
        functools.partial(branch, forward=True),
        functools.partial(branch, forward=False),
        tokens, cell_mask, shifts, projection_in, projection_out, cotangent,
    )


def solution(mesh):
    placed = (
        P(("groups", "fsdp"), "rows", None, None),
        P(("groups", "fsdp"), "rows", None),
        P(),
        P(("fsdp", "rows"), None),
        P(("fsdp", "rows"), None),
        P(("groups", "fsdp"), "rows", None, None),
    )
    return jax.shard_map(
        body,
        mesh=mesh,
        in_specs=placed,
        out_specs=(
            P(("groups", "fsdp"), "rows", None, None),
            P(("groups", "fsdp"), "rows", None, None),
            P(("groups", "fsdp", "rows"), None),
            P(("groups", "fsdp", "rows"), None),
        ),
        check_vma=False,
    )
```

```python
import functools

import jax
import jax.numpy as jnp
import numpy as np
from jax import lax
from jax.experimental import pallas as pl
from jax.experimental.pallas import tpu as pltpu
from jax.sharding import PartitionSpec as P

HEADS = 8
HD = 64
PAIR = 2 * HD
TILE = 16
F32 = jnp.float32
BF16 = jnp.bfloat16
VM = pl.BlockSpec(memory_space=pltpu.VMEM)
SM = pl.BlockSpec(memory_space=pltpu.SMEM)


def stage_masks(rows):
    bits = [1 << b for b in range(rows.bit_length() - 1)]
    far = bits[:1:-1]
    return (far + bits[:2], far + bits[:2][::-1])


def slot_masks(rows, core):
    masks = [0]
    for m in stage_masks(rows)[core]:
        masks = masks + [a ^ m for a in masks]
    return np.array(masks, np.int32)


def exchange(block, rows, stage):
    masks = stage_masks(rows)
    pairs = [
        (c * rows + i, c * rows + (i ^ masks[c][stage])) for c in range(2) for i in range(rows)
    ]
    return lax.ppermute(block, ("fsdp", "rows"), pairs)


def swap_cores(block):
    return lax.ppermute(block, "fsdp", [(0, 1), (1, 0)])


def shifted(block, rows, distance):
    return lax.ppermute(block, "rows", [((i - distance) % rows, i) for i in range(rows)])


def call(kernel, outs, specs, scratch=(), flops=0, moved=0, name=None):
    return pl.pallas_call(
        kernel,
        out_shape=tuple(jax.ShapeDtypeStruct(s, d) for s, d in outs),
        in_specs=list(specs),
        out_specs=tuple(VM for _ in outs),
        scratch_shapes=list(scratch),
        compiler_params=pltpu.CompilerParams(vmem_limit_bytes=40 << 20),
        cost_estimate=pl.CostEstimate(flops=flops, bytes_accessed=moved, transcendentals=0),
        name=name,
    )


def dot(a, b, ca=1, cb=0):
    return lax.dot_general(a, b, (((ca,), (cb,)), ((), ())), preferred_element_type=F32)


def place(full_in, full_out, piece, table, first, count):
    size = piece.shape[0] // count
    small = size // 2
    wide = full_in.shape[1]
    side = full_out.shape[1] // 2

    def step(j, carry):
        block = table[first + j]
        at = pl.multiple_of(block * size, size)
        at_out = pl.multiple_of(block * small, small)
        of = pl.multiple_of(j * size, size)
        full_in[pl.ds(at, size), :] = piece[pl.ds(of, size), pl.ds(0, wide)]
        for h in range(2):
            from_at = pl.multiple_of(of + h * small, small)
            full_out[pl.ds(at_out, small), pl.ds(h * side, side)] = piece[
                pl.ds(from_at, small), pl.ds(wide, side)
            ]
        return carry

    lax.fori_loop(0, count, step, 0)


def pick(dst, src, table, count, size):
    def step(j, carry):
        at = pl.multiple_of(table[j] * size, size)
        dst[pl.ds(pl.multiple_of(j * size, size), size), :] = src[pl.ds(at, size), :]
        return carry

    lax.fori_loop(0, count, step, 0)


def borrowed_rows(scal, low, count, cols, forward):
    row = (lax.broadcasted_iota(jnp.int32, (count, 1), 0) + low) // cols
    return row < scal[0] if forward else row >= scal[0]


def norm_kernel(scal, table, own, halo, xw, normed_bf, ordered, mean_out, inv_out, turned, *, low, cols, forward, blocks):
    half = halo.shape[0] - TILE
    take = borrowed_rows(scal, low, half, cols, forward)
    xw[...] = own[...]
    mixed = jnp.where(take, halo[pl.ds(0, half), :].astype(F32), own[pl.ds(low, half), :].astype(F32))
    xw[pl.ds(low, half), :] = mixed.astype(BF16)
    x = xw[...].astype(F32)
    mean = jnp.mean(x, axis=-1, keepdims=True)
    centered = x - mean
    inv = lax.rsqrt(jnp.mean(centered * centered, axis=-1, keepdims=True) + 1e-05)
    normed = centered * inv
    normed_bf[...] = normed.astype(BF16)
    mean_out[...] = mean
    inv_out[...] = inv
    turned[...] = normed.T.astype(BF16)
    pick(ordered, turned, table, blocks, turned.shape[0] // blocks)


def forward_kernel(place_at, order, normed_bf, bias, *refs, blocks):
    pieces, (full, full_out, packed, attn, ctx, ctx_ordered, turned) = refs[:-7], refs[-7:]
    each = blocks // len(pieces)
    for i, w in enumerate(pieces):
        place(full, full_out, w, place_at, i * each, each)
    hidden = ctx.shape[1]
    packed[...] = dot(normed_bf[...], full[...]).astype(BF16)
    cells = normed_bf.shape[0]
    first = lax.broadcasted_iota(jnp.int32, (cells, PAIR), 1) < HD
    def pair(p, carry):
        at = pl.multiple_of(p * PAIR, PAIR)
        q = packed[:, pl.ds(at, PAIR)].astype(F32)
        k = packed[:, pl.ds(pl.multiple_of(hidden + at, PAIR), PAIR)]
        v = packed[:, pl.ds(pl.multiple_of(2 * hidden + at, PAIR), PAIR)]
        parts = []
        for side in range(2):
            q_one = jnp.where(first if side == 0 else ~first, q, 0.0).astype(BF16)
            scores = dot(q_one, k, 1, 1) * (HD ** (-0.5)) + bias[...]
            e = jnp.exp(scores - jnp.max(scores, axis=-1, keepdims=True))
            a = e * (1.0 / jnp.sum(e, axis=-1, keepdims=True))
            attn[2 * p + side] = a
            parts.append(dot(a.astype(BF16), v))
        both = jnp.where(first, parts[0], parts[1])
        ctx[:, pl.ds(at, PAIR)] = both.astype(BF16)
        turned[pl.ds(at, PAIR), :] = both.T.astype(BF16)
        return carry

    lax.fori_loop(0, HEADS // 2, pair, 0)
    pick(ctx_ordered, turned, order, blocks, turned.shape[0] // blocks)


def term_out_kernel(scal, ctx_ordered, own, halo, cot, keep, send, *, low, cols, forward):
    half = halo.shape[0]
    take = borrowed_rows(scal, low, half, cols, forward)
    cot[...] = own[...]
    cot[pl.ds(low, half), :] = jnp.where(
        take, halo[...].astype(F32), own[pl.ds(low, half), :].astype(F32)
    ).astype(BF16)
    n = keep.shape[0]
    send[...] = dot(ctx_ordered[pl.ds(n, n), :], cot[...]).astype(BF16)
    keep[...] = dot(ctx_ordered[pl.ds(0, n), :], cot[...])


def half_backward(packed, attn, gctx, gp, first_pair, pairs):
    cells = packed.shape[0]
    hidden = packed.shape[1] // 3
    width = pairs * PAIR
    first = lax.broadcasted_iota(jnp.int32, (cells, PAIR), 1) < HD

    def pair(i, carry):
        at = pl.multiple_of(i * PAIR, PAIR)
        from_at = pl.multiple_of(first_pair * PAIR + at, PAIR)
        q = packed[:, pl.ds(from_at, PAIR)]
        k = packed[:, pl.ds(pl.multiple_of(hidden + from_at, PAIR), PAIR)]
        v = packed[:, pl.ds(pl.multiple_of(2 * hidden + from_at, PAIR), PAIR)]
        g = gctx[:, pl.ds(from_at, PAIR)]
        gf = g.astype(F32)
        gq, gk, gv = [], [], []
        for side in range(2):
            g_one = jnp.where(first if side == 0 else ~first, gf, 0.0).astype(BF16)
            a = attn[2 * (first_pair + i) + side]
            ga = dot(g_one, v, 1, 1)
            inner = jnp.sum(ga * a, axis=-1, keepdims=True)
            gs = (a * (ga - inner) * (HD ** (-0.5))).astype(BF16)
            gq.append(dot(gs, k))
            gk.append(dot(gs, q, 0, 0))
            gv.append(dot(a.astype(BF16), g, 0, 0))
        for t, two in enumerate((gq, gk, gv)):
            to = pl.multiple_of(t * width + at, PAIR)
            gp[:, pl.ds(to, PAIR)] = jnp.where(first, two[0], two[1]).astype(BF16)
        return carry

    lax.fori_loop(0, pairs, pair, 0)


def term_of(ordered, gp, keep, send):
    n = keep.shape[0]
    send[...] = dot(ordered[pl.ds(n, n), :], gp[...]).astype(BF16)
    keep[...] = dot(ordered[pl.ds(0, n), :], gp[...])


def backward_a_kernel(cot, packed, attn, ordered, full, gctx, gp, keep, send):
    gctx[...] = dot(cot[...], full[...], 1, 1).astype(BF16)
    half_backward(packed, attn, gctx, gp, 0, HEADS // 4)
    term_of(ordered, gp, keep, send)


def backward_b_kernel(packed, attn, gctx, ordered, gp, keep, send):
    half_backward(packed, attn, gctx, gp, HEADS // 4, HEADS // 4)
    term_of(ordered, gp, keep, send)


def grad_kernel(xw, mean, inv, gp_a, gp_b, full, cot, grad, gp):
    width = gp.shape[1] // 6
    for t in range(3):
        gp[:, pl.ds(2 * t * width, width)] = gp_a[:, pl.ds(t * width, width)]
        gp[:, pl.ds((2 * t + 1) * width, width)] = gp_b[:, pl.ds(t * width, width)]
    gn = dot(gp[...], full[...], 1, 1)
    normed = (xw[...].astype(F32) - mean[...]) * inv[...]
    m1 = jnp.mean(gn, axis=-1, keepdims=True)
    m2 = jnp.mean(gn * normed, axis=-1, keepdims=True)
    grad[...] = (cot[...].astype(F32) + inv[...] * (gn - m1 - normed * m2)).astype(BF16)


def output_kernel(scal, own, ctx, back, full, out, mixed, *, low, cols, forward):
    half = back.shape[0]
    take = borrowed_rows(scal, low, half, cols, forward)
    mixed[...] = ctx[...]
    mixed[pl.ds(low, half), :] = jnp.where(
        take, back[...].astype(F32), ctx[pl.ds(low, half), :].astype(F32)
    ).astype(BF16)
    out[...] = (own[...].astype(F32) + dot(mixed[...], full[...])).astype(BF16)


def after(value, *done):
    return lax.optimization_barrier((value, *done))[0]


def gather_pieces(shard, rows, halo):
    stages = len(stage_masks(rows)[0])
    own = shard
    for stage in range(stages - 3):
        own = jnp.concatenate([own, exchange(own, rows, stage)], axis=0)
    a, b, c = stages - 3, stages - 2, stages - 1
    got_a = exchange(own, rows, a)
    got_b = exchange(own, rows, b)
    got_c = exchange(own, rows, c)
    got_ab = exchange(after(got_a, got_b, halo), rows, b)
    got_ac = exchange(after(got_a, got_c), rows, c)
    got_bc = exchange(after(got_b, got_c), rows, c)
    got_abc = exchange(after(got_ab, got_ac), rows, c)
    held = (own, got_a, got_b, got_ab, got_c, got_ac, got_bc, got_abc)
    return held + tuple(swap_cores(x) for x in held)


def scatter_from(keep, arrived, rows):
    n = len(stage_masks(rows)[0])
    q = keep.shape[0] // 4
    keep = keep + arrived.astype(F32)
    first = keep[3 * q :].astype(BF16)
    far = exchange(first, rows, n - 1)
    near = exchange(keep[2 * q : 3 * q].astype(BF16), rows, n - 1)
    second = exchange((keep[q : 2 * q] + far.astype(F32)).astype(BF16), rows, n - 2)
    keep = keep[:q] + near.astype(F32) + second.astype(F32)
    for stage in range(n - 3, -1, -1):
        half = keep.shape[0] // 2
        arrived = exchange(keep[half:].astype(BF16), rows, stage)
        if stage:
            keep = keep[:half] + arrived.astype(F32)
    return keep[: keep.shape[0] // 2], arrived, first, (far, near, second)


def finish_kernel(keep_a, last_a, keep_b, last_b, out):
    fine = keep_a.shape[1] // 3
    for i, (keep, last) in enumerate(((keep_a, last_a), (keep_b, last_b))):
        for t in range(3):
            cols = pl.ds(t * fine, fine)
            out[:, pl.ds((2 * t + i) * fine, fine)] = keep[:, cols] + last[:, cols].astype(F32)


def branch(tokens, cell_mask, shifts, projection_in, projection_out, cotangent, *, forward, far_rows):
    rows = lax.axis_size("rows")
    row_count, cols, dim = tokens.shape[1:]
    cells = row_count * cols
    half = far_rows * cols
    hidden = HEADS * HD
    low = 0 if forward else cells - half
    distance = -1 if forward else 1
    core = lax.axis_index("fsdp")
    me = lax.axis_index("rows")
    blocks = 2 * rows
    m0 = jnp.asarray(slot_masks(rows, 0))
    m1 = jnp.asarray(slot_masks(rows, 1))
    mine = jnp.where(core == 0, m0, m1) ^ me
    theirs = jnp.where(core == 0, m1, m0) ^ me
    table = jnp.concatenate([core * rows + mine, (1 - core) * rows + theirs]).astype(jnp.int32)
    scal = shifts.astype(jnp.int32)
    s_row, s_col = scal[0], scal[1]
    part = lambda a: lax.slice_in_dim(a, low, low + half, axis=0)

    own = tokens.reshape(cells, dim)
    own_cot = cotangent.reshape(cells, dim)
    own_mask = cell_mask.astype(BF16).reshape(cells, 1)
    mask_rows = jnp.pad(part(own_mask).T, ((0, TILE - 1), (0, dim - half)))
    halo = shifted(jnp.concatenate([part(own), mask_rows], axis=0), rows, distance)
    flat_out = jnp.concatenate([projection_out[:, : dim // 2], projection_out[:, dim // 2 :]], axis=0)
    both = jnp.concatenate([projection_in, flat_out], axis=1)
    in_parts = gather_pieces(both, rows, halo)
    halo_cot = shifted(after(part(own_cot), in_parts[5], in_parts[6]), rows, distance)
    halo_mask = halo[half, :half][:, None]

    cell = jnp.arange(cells, dtype=jnp.int32)
    cell_row, cell_col = cell // cols, cell % cols
    from_other = (cell_row < s_row) if forward else (cell_row >= s_row)
    pad = ((low, cells - half - low), (0, 0))
    key_ok = jnp.where(from_other, jnp.pad(halo_mask, pad)[:, 0], own_mask[:, 0]) > 0
    at_wrap = me == (rows - 1 if forward else 0)
    region = 2 * ((cell_row < s_row) & at_wrap).astype(jnp.int32) + (cell_col < s_col).astype(
        jnp.int32
    )
    allowed = (region[:, None] == region[None, :]) & (
        key_ok[None, :] | (cell[:, None] == cell[None, :])
    )
    bias = jnp.where(allowed, 0.0, -1e30).astype(F32)

    shape_kw = dict(low=low, cols=cols, forward=forward)
    xw, normed_bf, ordered, mean, inv = call(
        functools.partial(norm_kernel, blocks=blocks, **shape_kw),
        [((cells, dim), BF16), ((cells, dim), BF16), ((dim, cells), BF16), ((cells, 1), F32), ((cells, 1), F32)],
        [SM, SM, VM, VM],
        [pltpu.VMEM((dim, cells), BF16)],
        flops=20 * cells * dim,
        moved=10 * cells * dim,
        name="norm",
    )(scal, table, own, halo)
    full_in, full_out, packed, attn, ctx, ctx_ordered = call(
        functools.partial(forward_kernel, blocks=blocks),
        [((dim, 3 * hidden), BF16), ((hidden, dim), BF16), ((cells, 3 * hidden), BF16), ((HEADS, cells, cells), F32), ((cells, hidden), BF16), ((hidden, cells), BF16)],
        [SM, SM, VM, VM] + [VM] * len(in_parts),
        [pltpu.VMEM((hidden, cells), BF16)],
        flops=6 * cells * dim * 3 * hidden,
        moved=10 << 20,
        name="fwd",
    )(table, table, normed_bf, bias, *in_parts)
    back_ctx = shifted(part(ctx), rows, -distance)
    cot, keep_out, send_out = call(
        functools.partial(term_out_kernel, **shape_kw),
        [((cells, dim), BF16), ((hidden // 2, dim), F32), ((hidden // 2, dim), BF16)],
        [SM, VM, VM, VM],
        flops=2 * cells * dim * hidden,
        moved=4 << 20,
        name="term_out",
    )(scal, ctx_ordered, own_cot, halo_cot)
    swapped_out = swap_cores(send_out)
    quart = 3 * hidden // 2
    half_outs = [((cells, quart), BF16), ((dim // 2, quart), F32), ((dim // 2, quart), BF16)]
    gctx, gp_a, keep_a, send_a = call(
        backward_a_kernel,
        [((cells, hidden), BF16)] + half_outs,
        [VM] * 5,
        flops=4 * cells * dim * 3 * hidden,
        moved=6 << 20,
        name="bwd_a",
    )(cot, packed, attn, ordered, full_out)
    swapped_a = swap_cores(send_a)
    gp_b, keep_b, send_b = call(
        backward_b_kernel,
        half_outs,
        [VM, VM, VM, VM],
        flops=4 * cells * dim * 3 * hidden,
        moved=6 << 20,
        name="bwd_b",
    )(packed, attn, after(gctx, swapped_out, back_ctx), ordered)
    swapped_b = swap_cores(send_b)
    kept_out, last_out, _, _ = scatter_from(keep_out, swapped_out, rows)
    grad_out = kept_out + last_out.astype(F32)
    kept_a, last_a, first_a, seen_a = scatter_from(keep_a, swapped_a, rows)
    kept_b, last_b, _, _ = scatter_from(keep_b, swapped_b, rows)
    (grad_in,) = call(
        finish_kernel,
        [((dim // blocks, 3 * hidden), F32)],
        [VM] * 4,
        moved=1 << 20,
        name="finish",
    )(kept_a, last_a, kept_b, last_b)
    (grad_win,) = call(
        grad_kernel,
        [((cells, dim), BF16)],
        [VM] * 7,
        [pltpu.VMEM((cells, 3 * hidden), BF16)],
        flops=2 * cells * dim * 3 * hidden,
        moved=6 << 20,
        name="grad",
    )(xw, mean, inv, gp_a, after(gp_b, first_a), full_in, cot)
    back_grad = shifted(part(grad_win), rows, -distance)
    (output,) = call(
        functools.partial(output_kernel, **shape_kw),
        [((cells, dim), BF16)],
        [SM, VM, VM, VM, VM],
        [pltpu.VMEM((cells, hidden), BF16)],
        flops=2 * cells * dim * hidden,
        moved=3 << 20,
        name="output",
    )(scal, own, ctx, after(back_ctx, seen_a[0]), full_out)
    own_grad = jnp.where(from_other[:, None], jnp.pad(back_grad, pad), grad_win)
    shape = tokens.shape
    return (output.reshape(shape), own_grad.reshape(shape), grad_in, grad_out)


def body(tokens, cell_mask, shifts, projection_in, projection_out, cotangent):
    rows, shift = tokens.shape[1], shifts[0]
    half, quarter = rows // 2, rows // 4
    behind = (shift > half).astype(jnp.int32)
    small = (jnp.minimum(shift, rows - shift) <= quarter).astype(jnp.int32)
    return lax.switch(
        2 * behind + small,
        [
            functools.partial(branch, forward=forward, far_rows=far)
            for forward in (True, False)
            for far in (half, quarter)
        ],
        tokens, cell_mask, shifts, projection_in, projection_out, cotangent,
    )


def solution(mesh):
    placed = (
        P(("groups", "fsdp"), "rows", None, None),
        P(("groups", "fsdp"), "rows", None),
        P(),
        P(("fsdp", "rows"), None),
        P(("fsdp", "rows"), None),
        P(("groups", "fsdp"), "rows", None, None),
    )
    return jax.shard_map(
        body,
        mesh=mesh,
        in_specs=placed,
        out_specs=(
            P(("groups", "fsdp"), "rows", None, None),
            P(("groups", "fsdp"), "rows", None, None),
            P(("groups", "fsdp", "rows"), None),
            P(("groups", "fsdp", "rows"), None),
        ),
        check_vma=False,
    )
```

```python
import functools

import jax
import jax.numpy as jnp
import numpy as np
from jax import lax
from jax.experimental import pallas as pl
from jax.experimental.pallas import tpu as pltpu
from jax.sharding import PartitionSpec as P

HEADS = 8
HD = 64
PAIR = 2 * HD
F32 = jnp.float32
BF16 = jnp.bfloat16
VM = pl.BlockSpec(memory_space=pltpu.VMEM)
SM = pl.BlockSpec(memory_space=pltpu.SMEM)


def stage_masks(rows):
    bits = [1 << b for b in range(rows.bit_length() - 1)]
    far = bits[:1:-1]
    return (far + bits[:2], far + bits[:2][::-1])


def slot_masks(rows, core):
    masks = [0]
    for m in stage_masks(rows)[core]:
        masks = masks + [a ^ m for a in masks]
    return np.array(masks, np.int32)


def exchange(block, rows, stage):
    masks = stage_masks(rows)
    pairs = [
        (c * rows + i, c * rows + (i ^ masks[c][stage])) for c in range(2) for i in range(rows)
    ]
    return lax.ppermute(block, ("fsdp", "rows"), pairs)


def swap_cores(block):
    return lax.ppermute(block, "fsdp", [(0, 1), (1, 0)])


def shifted(block, rows, distance):
    return lax.ppermute(block, "rows", [((i - distance) % rows, i) for i in range(rows)])


def call(kernel, outs, specs, scratch=(), flops=0, moved=0, name=None):
    return pl.pallas_call(
        kernel,
        out_shape=tuple(jax.ShapeDtypeStruct(s, d) for s, d in outs),
        in_specs=list(specs),
        out_specs=tuple(VM for _ in outs),
        scratch_shapes=list(scratch),
        compiler_params=pltpu.CompilerParams(vmem_limit_bytes=40 << 20),
        cost_estimate=pl.CostEstimate(flops=flops, bytes_accessed=moved, transcendentals=0),
        name=name,
    )


def dot(a, b, ca=1, cb=0):
    return lax.dot_general(a, b, (((ca,), (cb,)), ((), ())), preferred_element_type=F32)


def place(full_in, full_out, piece, table, first, count):
    size = piece.shape[0] // count
    small = size // 2
    wide = full_in.shape[1]
    side = full_out.shape[1] // 2

    def step(j, carry):
        block = table[first + j]
        at = pl.multiple_of(block * size, size)
        at_out = pl.multiple_of(block * small, small)
        of = pl.multiple_of(j * size, size)
        full_in[pl.ds(at, size), :] = piece[pl.ds(of, size), pl.ds(0, wide)]
        for h in range(2):
            from_at = pl.multiple_of(of + h * small, small)
            full_out[pl.ds(at_out, small), pl.ds(h * side, side)] = piece[
                pl.ds(from_at, small), pl.ds(wide, side)
            ]
        return carry

    lax.fori_loop(0, count, step, 0)


def pick(dst, src, table, count, size):
    def step(j, carry):
        at = pl.multiple_of(table[j] * size, size)
        dst[pl.ds(pl.multiple_of(j * size, size), size), :] = src[pl.ds(at, size), :]
        return carry

    lax.fori_loop(0, count, step, 0)


def borrowed_rows(scal, low, count, cols, forward):
    row = (lax.broadcasted_iota(jnp.int32, (count, 1), 0) + low) // cols
    return row < scal[0] if forward else row >= scal[0]


def norm_kernel(scal, table, own, halo, xw, normed_bf, ordered, mean_out, inv_out, turned, *, low, cols, forward, blocks):
    half = own.shape[0] // 2
    take = borrowed_rows(scal, low, half, cols, forward)
    keep_low = half - low
    xw[pl.ds(keep_low, half), :] = own[pl.ds(keep_low, half), :]
    mixed = jnp.where(take, halo[pl.ds(0, half), :].astype(F32), own[pl.ds(low, half), :].astype(F32))
    xw[pl.ds(low, half), :] = mixed.astype(BF16)
    x = xw[...].astype(F32)
    mean = jnp.mean(x, axis=-1, keepdims=True)
    centered = x - mean
    inv = lax.rsqrt(jnp.mean(centered * centered, axis=-1, keepdims=True) + 1e-05)
    normed = centered * inv
    normed_bf[...] = normed.astype(BF16)
    mean_out[...] = mean
    inv_out[...] = inv
    turned[...] = normed.T.astype(BF16)
    pick(ordered, turned, table, blocks, turned.shape[0] // blocks)


def forward_kernel(place_at, order, normed_bf, bias, *refs, blocks):
    pieces, (full, full_out, packed, attn, ctx, ctx_ordered, turned) = refs[:-7], refs[-7:]
    each = blocks // len(pieces)
    for i, w in enumerate(pieces):
        place(full, full_out, w, place_at, i * each, each)
    hidden = ctx.shape[1]
    packed[...] = dot(normed_bf[...], full[...]).astype(BF16)
    cells = normed_bf.shape[0]
    first = lax.broadcasted_iota(jnp.int32, (cells, PAIR), 1) < HD
    for p in range(HEADS // 2):
        lanes = pl.ds(p * PAIR, PAIR)
        q = packed[:, lanes].astype(F32)
        k = packed[:, pl.ds(hidden + p * PAIR, PAIR)]
        v = packed[:, pl.ds(2 * hidden + p * PAIR, PAIR)]
        parts = []
        for side in range(2):
            q_one = jnp.where(first if side == 0 else ~first, q, 0.0).astype(BF16)
            scores = dot(q_one, k, 1, 1) * (HD ** (-0.5)) + bias[...]
            e = jnp.exp(scores - jnp.max(scores, axis=-1, keepdims=True))
            a = e * (1.0 / jnp.sum(e, axis=-1, keepdims=True))
            attn[2 * p + side] = a
            parts.append(dot(a.astype(BF16), v))
        both = jnp.where(first, parts[0], parts[1])
        ctx[:, lanes] = both.astype(BF16)
        turned[lanes, :] = both.T.astype(BF16)
    pick(ctx_ordered, turned, order, blocks, turned.shape[0] // blocks)


def term_out_kernel(scal, ctx_ordered, own, halo, cot, keep, send, *, low, cols, forward):
    half = halo.shape[0]
    take = borrowed_rows(scal, low, half, cols, forward)
    keep_low = half - low
    cot[pl.ds(keep_low, half), :] = own[pl.ds(keep_low, half), :]
    cot[pl.ds(low, half), :] = jnp.where(
        take, halo[...].astype(F32), own[pl.ds(low, half), :].astype(F32)
    ).astype(BF16)
    n = keep.shape[0]
    send[...] = dot(ctx_ordered[pl.ds(n, n), :], cot[...]).astype(BF16)
    keep[...] = dot(ctx_ordered[pl.ds(0, n), :], cot[...])


def half_backward(packed, attn, gctx, gp, first_pair, pairs):
    cells = packed.shape[0]
    hidden = packed.shape[1] // 3
    width = pairs * PAIR
    first = lax.broadcasted_iota(jnp.int32, (cells, PAIR), 1) < HD
    for i in range(pairs):
        p = first_pair + i
        q = packed[:, pl.ds(p * PAIR, PAIR)]
        k = packed[:, pl.ds(hidden + p * PAIR, PAIR)]
        v = packed[:, pl.ds(2 * hidden + p * PAIR, PAIR)]
        g = gctx[:, pl.ds(p * PAIR, PAIR)]
        gf = g.astype(F32)
        gq, gk, gv = [], [], []
        for side in range(2):
            g_one = jnp.where(first if side == 0 else ~first, gf, 0.0).astype(BF16)
            a = attn[2 * p + side]
            ga = dot(g_one, v, 1, 1)
            inner = jnp.sum(ga * a, axis=-1, keepdims=True)
            gs = (a * (ga - inner) * (HD ** (-0.5))).astype(BF16)
            gq.append(dot(gs, k))
            gk.append(dot(gs, q, 0, 0))
            gv.append(dot(a.astype(BF16), g, 0, 0))
        for t, two in enumerate((gq, gk, gv)):
            gp[:, pl.ds(t * width + i * PAIR, PAIR)] = jnp.where(first, two[0], two[1]).astype(BF16)


def term_of(ordered, gp, keep, send):
    n = keep.shape[0]
    send[...] = dot(ordered[pl.ds(n, n), :], gp[...]).astype(BF16)
    keep[...] = dot(ordered[pl.ds(0, n), :], gp[...])


def backward_a_kernel(cot, packed, attn, ordered, full, gctx, gp, keep, send):
    gctx[...] = dot(cot[...], full[...], 1, 1).astype(BF16)
    half_backward(packed, attn, gctx, gp, 0, HEADS // 4)
    term_of(ordered, gp, keep, send)


def backward_b_kernel(packed, attn, gctx, ordered, gp, keep, send):
    half_backward(packed, attn, gctx, gp, HEADS // 4, HEADS // 4)
    term_of(ordered, gp, keep, send)


def grad_kernel(xw, mean, inv, gp_a, gp_b, full, cot, grad, gp):
    width = gp.shape[1] // 6
    for t in range(3):
        gp[:, pl.ds(2 * t * width, width)] = gp_a[:, pl.ds(t * width, width)]
        gp[:, pl.ds((2 * t + 1) * width, width)] = gp_b[:, pl.ds(t * width, width)]
    gn = dot(gp[...], full[...], 1, 1)
    normed = (xw[...].astype(F32) - mean[...]) * inv[...]
    m1 = jnp.mean(gn, axis=-1, keepdims=True)
    m2 = jnp.mean(gn * normed, axis=-1, keepdims=True)
    grad[...] = (cot[...].astype(F32) + inv[...] * (gn - m1 - normed * m2)).astype(BF16)


def output_kernel(scal, own, ctx, back, full, out, mixed, *, low, cols, forward):
    half = back.shape[0]
    take = borrowed_rows(scal, low, half, cols, forward)
    keep_low = half - low
    mixed[pl.ds(keep_low, half), :] = ctx[pl.ds(keep_low, half), :]
    mixed[pl.ds(low, half), :] = jnp.where(
        take, back[...].astype(F32), ctx[pl.ds(low, half), :].astype(F32)
    ).astype(BF16)
    out[...] = (own[...].astype(F32) + dot(mixed[...], full[...])).astype(BF16)


def after(value, *done):
    return lax.optimization_barrier((value, *done))[0]


def gather_pieces(shard, rows, halo):
    stages = len(stage_masks(rows)[0])
    own = shard
    for stage in range(stages - 3):
        own = jnp.concatenate([own, exchange(own, rows, stage)], axis=0)
    a, b, c = stages - 3, stages - 2, stages - 1
    got_a = exchange(own, rows, a)
    got_b = exchange(own, rows, b)
    got_c = exchange(own, rows, c)
    got_ab = exchange(after(got_a, got_b, halo), rows, b)
    got_ac = exchange(after(got_a, got_c), rows, c)
    got_bc = exchange(after(got_b, got_c), rows, c)
    got_abc = exchange(after(got_ab, got_ac), rows, c)
    held = (own, got_a, got_b, got_ab, got_c, got_ac, got_bc, got_abc)
    return held + tuple(swap_cores(x) for x in held)


def scatter_from(keep, arrived, rows):
    n = len(stage_masks(rows)[0])
    q = keep.shape[0] // 4
    keep = keep + arrived.astype(F32)
    first = keep[2 * q :].astype(BF16)
    h = 2 * q
    far = exchange(keep[h:].astype(BF16), rows, n - 1)
    keep = keep[:h] + far.astype(F32)
    near = second = exchange(keep[q:].astype(BF16), rows, n - 2)
    keep = keep[:q] + second.astype(F32)
    for stage in range(n - 3, -1, -1):
        half = keep.shape[0] // 2
        arrived = exchange(keep[half:].astype(BF16), rows, stage)
        if stage:
            keep = keep[:half] + arrived.astype(F32)
    return keep[: keep.shape[0] // 2], arrived, first, (far, near, second)


def finish_kernel(keep_a, last_a, keep_b, last_b, out):
    fine = keep_a.shape[1] // 3
    for i, (keep, last) in enumerate(((keep_a, last_a), (keep_b, last_b))):
        for t in range(3):
            cols = pl.ds(t * fine, fine)
            out[:, pl.ds((2 * t + i) * fine, fine)] = keep[:, cols] + last[:, cols].astype(F32)


def branch(tokens, cell_mask, shifts, projection_in, projection_out, cotangent, *, forward):
    rows = lax.axis_size("rows")
    row_count, cols, dim = tokens.shape[1:]
    cells = row_count * cols
    half = cells // 2
    hidden = HEADS * HD
    low = 0 if forward else half
    distance = -1 if forward else 1
    core = lax.axis_index("fsdp")
    me = lax.axis_index("rows")
    blocks = 2 * rows
    m0 = jnp.asarray(slot_masks(rows, 0))
    m1 = jnp.asarray(slot_masks(rows, 1))
    mine = jnp.where(core == 0, m0, m1) ^ me
    theirs = jnp.where(core == 0, m1, m0) ^ me
    table = jnp.concatenate([core * rows + mine, (1 - core) * rows + theirs]).astype(jnp.int32)
    scal = shifts.astype(jnp.int32)
    s_row, s_col = scal[0], scal[1]
    part = lambda a: lax.slice_in_dim(a, low, low + half, axis=0)

    own = tokens.reshape(cells, dim)
    own_cot = cotangent.reshape(cells, dim)
    own_mask = cell_mask.astype(BF16).reshape(cells, 1)
    tile = 16
    mask_rows = jnp.pad(part(own_mask).T, ((0, tile - 1), (0, dim - half)))
    halo = shifted(jnp.concatenate([part(own), mask_rows], axis=0), rows, distance)
    flat_out = jnp.concatenate([projection_out[:, : dim // 2], projection_out[:, dim // 2 :]], axis=0)
    both = jnp.concatenate([projection_in, flat_out], axis=1)
    in_parts = gather_pieces(both, rows, halo)
    halo_cot = shifted(after(part(own_cot), in_parts[5], in_parts[6]), rows, distance)
    halo_mask = halo[half, :half][:, None]

    cell = jnp.arange(cells, dtype=jnp.int32)
    cell_row, cell_col = cell // cols, cell % cols
    from_other = (cell_row < s_row) if forward else (cell_row >= s_row)
    pad = ((low, half - low), (0, 0))
    key_ok = jnp.where(from_other, jnp.pad(halo_mask, pad)[:, 0], own_mask[:, 0]) > 0
    at_wrap = me == (rows - 1 if forward else 0)
    region = 2 * ((cell_row < s_row) & at_wrap).astype(jnp.int32) + (cell_col < s_col).astype(
        jnp.int32
    )
    allowed = (region[:, None] == region[None, :]) & (
        key_ok[None, :] | (cell[:, None] == cell[None, :])
    )
    bias = jnp.where(allowed, 0.0, -1e30).astype(F32)

    shape_kw = dict(low=low, cols=cols, forward=forward)
    xw, normed_bf, ordered, mean, inv = call(
        functools.partial(norm_kernel, blocks=blocks, **shape_kw),
        [((cells, dim), BF16), ((cells, dim), BF16), ((dim, cells), BF16), ((cells, 1), F32), ((cells, 1), F32)],
        [SM, SM, VM, VM],
        [pltpu.VMEM((dim, cells), BF16)],
        flops=20 * cells * dim,
        moved=10 * cells * dim,
        name="norm",
    )(scal, table, own, halo)
    full_in, full_out, packed, attn, ctx, ctx_ordered = call(
        functools.partial(forward_kernel, blocks=blocks),
        [((dim, 3 * hidden), BF16), ((hidden, dim), BF16), ((cells, 3 * hidden), BF16), ((HEADS, cells, cells), F32), ((cells, hidden), BF16), ((hidden, cells), BF16)],
        [SM, SM, VM, VM] + [VM] * len(in_parts),
        [pltpu.VMEM((hidden, cells), BF16)],
        flops=6 * cells * dim * 3 * hidden,
        moved=10 << 20,
        name="fwd",
    )(table, table, normed_bf, bias, *in_parts)
    back_ctx = shifted(part(ctx), rows, -distance)
    cot, keep_out, send_out = call(
        functools.partial(term_out_kernel, **shape_kw),
        [((cells, dim), BF16), ((hidden // 2, dim), F32), ((hidden // 2, dim), BF16)],
        [SM, VM, VM, VM],
        flops=2 * cells * dim * hidden,
        moved=4 << 20,
        name="term_out",
    )(scal, ctx_ordered, own_cot, halo_cot)
    swapped_out = swap_cores(send_out)
    quart = 3 * hidden // 2
    half_outs = [((cells, quart), BF16), ((dim // 2, quart), F32), ((dim // 2, quart), BF16)]
    gctx, gp_a, keep_a, send_a = call(
        backward_a_kernel,
        [((cells, hidden), BF16)] + half_outs,
        [VM] * 5,
        flops=4 * cells * dim * 3 * hidden,
        moved=6 << 20,
        name="bwd_a",
    )(cot, packed, attn, ordered, full_out)
    swapped_a = swap_cores(send_a)
    gp_b, keep_b, send_b = call(
        backward_b_kernel,
        half_outs,
        [VM, VM, VM, VM],
        flops=4 * cells * dim * 3 * hidden,
        moved=6 << 20,
        name="bwd_b",
    )(packed, attn, after(gctx, swapped_out, back_ctx), ordered)
    swapped_b = swap_cores(send_b)
    kept_out, last_out, _, _ = scatter_from(keep_out, swapped_out, rows)
    grad_out = kept_out + last_out.astype(F32)
    kept_a, last_a, first_a, seen_a = scatter_from(keep_a, swapped_a, rows)
    kept_b, last_b, _, _ = scatter_from(keep_b, swapped_b, rows)
    (grad_in,) = call(
        finish_kernel,
        [((dim // blocks, 3 * hidden), F32)],
        [VM] * 4,
        moved=1 << 20,
        name="finish",
    )(kept_a, last_a, kept_b, last_b)
    (grad_win,) = call(
        grad_kernel,
        [((cells, dim), BF16)],
        [VM] * 7,
        [pltpu.VMEM((cells, 3 * hidden), BF16)],
        flops=2 * cells * dim * 3 * hidden,
        moved=6 << 20,
        name="grad",
    )(xw, mean, inv, gp_a, after(gp_b, first_a), full_in, cot)
    back_grad = shifted(part(grad_win), rows, -distance)
    (output,) = call(
        functools.partial(output_kernel, **shape_kw),
        [((cells, dim), BF16)],
        [SM, VM, VM, VM, VM],
        [pltpu.VMEM((cells, hidden), BF16)],
        flops=2 * cells * dim * hidden,
        moved=3 << 20,
        name="output",
    )(scal, own, ctx, after(back_ctx, seen_a[0]), full_out)
    own_grad = jnp.where(from_other[:, None], jnp.pad(back_grad, pad), grad_win)
    shape = tokens.shape
    return (output.reshape(shape), own_grad.reshape(shape), grad_in, grad_out)


def body(tokens, cell_mask, shifts, projection_in, projection_out, cotangent):
    return lax.cond(
        shifts[0] <= tokens.shape[1] // 2,
        functools.partial(branch, forward=True),
        functools.partial(branch, forward=False),
        tokens, cell_mask, shifts, projection_in, projection_out, cotangent,
    )


def solution(mesh):
    placed = (
        P(("groups", "fsdp"), "rows", None, None),
        P(("groups", "fsdp"), "rows", None),
        P(),
        P(("fsdp", "rows"), None),
        P(("fsdp", "rows"), None),
        P(("groups", "fsdp"), "rows", None, None),
    )
    return jax.shard_map(
        body,
        mesh=mesh,
        in_specs=placed,
        out_specs=(
            P(("groups", "fsdp"), "rows", None, None),
            P(("groups", "fsdp"), "rows", None, None),
            P(("groups", "fsdp", "rows"), None),
            P(("groups", "fsdp", "rows"), None),
        ),
        check_vma=False,
    )
```

```python
import functools

import jax
import jax.numpy as jnp
import numpy as np
from jax import lax
from jax.experimental import pallas as pl
from jax.experimental.pallas import tpu as pltpu
from jax.sharding import PartitionSpec as P

HEADS = 8
HD = 64
PAIR = 2 * HD
F32 = jnp.float32
BF16 = jnp.bfloat16
VM = pl.BlockSpec(memory_space=pltpu.VMEM)
SM = pl.BlockSpec(memory_space=pltpu.SMEM)


def stage_masks(rows):
    bits = [1 << b for b in range(rows.bit_length() - 1)]
    far = bits[:1:-1]
    return (far + bits[:2], far + bits[:2][::-1])


def slot_masks(rows, core):
    masks = [0]
    for m in stage_masks(rows)[core]:
        masks = masks + [a ^ m for a in masks]
    return np.array(masks, np.int32)


def exchange(block, rows, stage):
    masks = stage_masks(rows)
    pairs = [
        (c * rows + i, c * rows + (i ^ masks[c][stage])) for c in range(2) for i in range(rows)
    ]
    return lax.ppermute(block, ("fsdp", "rows"), pairs)


def swap_cores(block):
    return lax.ppermute(block, "fsdp", [(0, 1), (1, 0)])


def shifted(block, rows, distance):
    return lax.ppermute(block, "rows", [((i - distance) % rows, i) for i in range(rows)])


def call(kernel, outs, specs, scratch=(), flops=0, moved=0, name=None):
    return pl.pallas_call(
        kernel,
        out_shape=tuple(jax.ShapeDtypeStruct(s, d) for s, d in outs),
        in_specs=list(specs),
        out_specs=tuple(VM for _ in outs),
        scratch_shapes=list(scratch),
        compiler_params=pltpu.CompilerParams(vmem_limit_bytes=40 << 20),
        cost_estimate=pl.CostEstimate(flops=flops, bytes_accessed=moved, transcendentals=0),
        name=name,
    )


def dot(a, b, ca=1, cb=0):
    return lax.dot_general(a, b, (((ca,), (cb,)), ((), ())), preferred_element_type=F32)


def place(full_in, full_out, piece, table, first, count):
    size = piece.shape[0] // count
    small = size // 2
    wide = full_in.shape[1]
    side = full_out.shape[1] // 2

    def step(j, carry):
        block = table[first + j]
        at = pl.multiple_of(block * size, size)
        at_out = pl.multiple_of(block * small, small)
        of = pl.multiple_of(j * size, size)
        full_in[pl.ds(at, size), :] = piece[pl.ds(of, size), pl.ds(0, wide)]
        for h in range(2):
            from_at = pl.multiple_of(of + h * small, small)
            full_out[pl.ds(at_out, small), pl.ds(h * side, side)] = piece[
                pl.ds(from_at, small), pl.ds(wide, side)
            ]
        return carry

    lax.fori_loop(0, count, step, 0)


def pick(dst, src, table, count, size):
    def step(j, carry):
        at = pl.multiple_of(table[j] * size, size)
        dst[pl.ds(pl.multiple_of(j * size, size), size), :] = src[pl.ds(at, size), :]
        return carry

    lax.fori_loop(0, count, step, 0)


def borrowed_rows(scal, low, count, cols, forward):
    row = (lax.broadcasted_iota(jnp.int32, (count, 1), 0) + low) // cols
    return row < scal[0] if forward else row >= scal[0]


def norm_kernel(scal, table, own, halo, xw, normed_bf, ordered, mean_out, inv_out, turned, *, low, cols, forward, blocks):
    half = own.shape[0] // 2
    take = borrowed_rows(scal, low, half, cols, forward)
    keep_low = half - low
    xw[pl.ds(keep_low, half), :] = own[pl.ds(keep_low, half), :]
    mixed = jnp.where(take, halo[pl.ds(0, half), :].astype(F32), own[pl.ds(low, half), :].astype(F32))
    xw[pl.ds(low, half), :] = mixed.astype(BF16)
    x = xw[...].astype(F32)
    mean = jnp.mean(x, axis=-1, keepdims=True)
    centered = x - mean
    inv = lax.rsqrt(jnp.mean(centered * centered, axis=-1, keepdims=True) + 1e-05)
    normed = centered * inv
    normed_bf[...] = normed.astype(BF16)
    mean_out[...] = mean
    inv_out[...] = inv
    turned[...] = normed.T.astype(BF16)
    pick(ordered, turned, table, blocks, turned.shape[0] // blocks)


def forward_kernel(place_at, order, normed_bf, bias, *refs, blocks):
    pieces, (full, full_out, packed, attn, ctx, ctx_ordered, turned) = refs[:-7], refs[-7:]
    each = blocks // len(pieces)
    for i, w in enumerate(pieces):
        place(full, full_out, w, place_at, i * each, each)
    hidden = ctx.shape[1]
    packed[...] = dot(normed_bf[...], full[...]).astype(BF16)
    cells = normed_bf.shape[0]
    first = lax.broadcasted_iota(jnp.int32, (cells, PAIR), 1) < HD
    for p in range(HEADS // 2):
        lanes = pl.ds(p * PAIR, PAIR)
        q = packed[:, lanes].astype(F32)
        k = packed[:, pl.ds(hidden + p * PAIR, PAIR)]
        v = packed[:, pl.ds(2 * hidden + p * PAIR, PAIR)]
        parts = []
        for side in range(2):
            q_one = jnp.where(first if side == 0 else ~first, q, 0.0).astype(BF16)
            scores = dot(q_one, k, 1, 1) * (HD ** (-0.5)) + bias[...]
            e = jnp.exp(scores - jnp.max(scores, axis=-1, keepdims=True))
            a = e * (1.0 / jnp.sum(e, axis=-1, keepdims=True))
            attn[2 * p + side] = a
            parts.append(dot(a.astype(BF16), v))
        both = jnp.where(first, parts[0], parts[1])
        ctx[:, lanes] = both.astype(BF16)
        turned[lanes, :] = both.T.astype(BF16)
    pick(ctx_ordered, turned, order, blocks, turned.shape[0] // blocks)


def term_out_kernel(scal, ctx_ordered, own, halo, cot, keep, send, *, low, cols, forward):
    half = halo.shape[0]
    take = borrowed_rows(scal, low, half, cols, forward)
    keep_low = half - low
    cot[pl.ds(keep_low, half), :] = own[pl.ds(keep_low, half), :]
    cot[pl.ds(low, half), :] = jnp.where(
        take, halo[...].astype(F32), own[pl.ds(low, half), :].astype(F32)
    ).astype(BF16)
    n = keep.shape[0]
    send[...] = dot(ctx_ordered[pl.ds(n, n), :], cot[...]).astype(BF16)
    keep[...] = dot(ctx_ordered[pl.ds(0, n), :], cot[...])


def half_backward(packed, attn, gctx, gp, first_pair, pairs):
    cells = packed.shape[0]
    hidden = packed.shape[1] // 3
    width = pairs * PAIR
    first = lax.broadcasted_iota(jnp.int32, (cells, PAIR), 1) < HD
    for i in range(pairs):
        p = first_pair + i
        q = packed[:, pl.ds(p * PAIR, PAIR)]
        k = packed[:, pl.ds(hidden + p * PAIR, PAIR)]
        v = packed[:, pl.ds(2 * hidden + p * PAIR, PAIR)]
        g = gctx[:, pl.ds(p * PAIR, PAIR)]
        gf = g.astype(F32)
        gq, gk, gv = [], [], []
        for side in range(2):
            g_one = jnp.where(first if side == 0 else ~first, gf, 0.0).astype(BF16)
            a = attn[2 * p + side]
            ga = dot(g_one, v, 1, 1)
            inner = jnp.sum(ga * a, axis=-1, keepdims=True)
            gs = (a * (ga - inner) * (HD ** (-0.5))).astype(BF16)
            gq.append(dot(gs, k))
            gk.append(dot(gs, q, 0, 0))
            gv.append(dot(a.astype(BF16), g, 0, 0))
        for t, two in enumerate((gq, gk, gv)):
            gp[:, pl.ds(t * width + i * PAIR, PAIR)] = jnp.where(first, two[0], two[1]).astype(BF16)


def term_of(ordered, gp, keep, send):
    n = keep.shape[0]
    send[...] = dot(ordered[pl.ds(n, n), :], gp[...]).astype(BF16)
    keep[...] = dot(ordered[pl.ds(0, n), :], gp[...])


def backward_a_kernel(cot, packed, attn, ordered, full, gctx, gp, keep, send):
    gctx[...] = dot(cot[...], full[...], 1, 1).astype(BF16)
    half_backward(packed, attn, gctx, gp, 0, HEADS // 4)
    term_of(ordered, gp, keep, send)


def backward_b_kernel(packed, attn, gctx, ordered, gp, keep, send):
    half_backward(packed, attn, gctx, gp, HEADS // 4, HEADS // 4)
    term_of(ordered, gp, keep, send)


def grad_kernel(xw, mean, inv, gp_a, gp_b, full, cot, grad, gp):
    width = gp.shape[1] // 6
    for t in range(3):
        gp[:, pl.ds(2 * t * width, width)] = gp_a[:, pl.ds(t * width, width)]
        gp[:, pl.ds((2 * t + 1) * width, width)] = gp_b[:, pl.ds(t * width, width)]
    gn = dot(gp[...], full[...], 1, 1)
    normed = (xw[...].astype(F32) - mean[...]) * inv[...]
    m1 = jnp.mean(gn, axis=-1, keepdims=True)
    m2 = jnp.mean(gn * normed, axis=-1, keepdims=True)
    grad[...] = (cot[...].astype(F32) + inv[...] * (gn - m1 - normed * m2)).astype(BF16)


def output_kernel(scal, own, ctx, back, full, out, mixed, *, low, cols, forward):
    half = back.shape[0]
    take = borrowed_rows(scal, low, half, cols, forward)
    keep_low = half - low
    mixed[pl.ds(keep_low, half), :] = ctx[pl.ds(keep_low, half), :]
    mixed[pl.ds(low, half), :] = jnp.where(
        take, back[...].astype(F32), ctx[pl.ds(low, half), :].astype(F32)
    ).astype(BF16)
    out[...] = (own[...].astype(F32) + dot(mixed[...], full[...])).astype(BF16)


def after(value, *done):
    return lax.optimization_barrier((value, *done))[0]


def gather_pieces(shard, rows, halo):
    stages = len(stage_masks(rows)[0])
    own = shard
    for stage in range(stages - 3):
        own = jnp.concatenate([own, exchange(own, rows, stage)], axis=0)
    a, b, c = stages - 3, stages - 2, stages - 1
    got_a = exchange(own, rows, a)
    got_b = exchange(own, rows, b)
    got_c = exchange(own, rows, c)
    got_ab = exchange(after(got_a, got_b), rows, b)
    got_ac = exchange(after(got_a, got_c), rows, c)
    got_bc = exchange(after(got_b, got_c), rows, c)
    got_abc = exchange(after(got_ab, got_ac, halo), rows, c)
    held = (own, got_a, got_b, got_ab, got_c, got_ac, got_bc, got_abc)
    return held + tuple(swap_cores(x) for x in held)


def scatter_from(keep, arrived, rows):
    n = len(stage_masks(rows)[0])
    q = keep.shape[0] // 4
    keep = keep + arrived.astype(F32)
    first = keep[2 * q :].astype(BF16)
    h = 2 * q
    far = exchange(keep[h:].astype(BF16), rows, n - 1)
    keep = keep[:h] + far.astype(F32)
    near = second = exchange(keep[q:].astype(BF16), rows, n - 2)
    keep = keep[:q] + second.astype(F32)
    for stage in range(n - 3, -1, -1):
        half = keep.shape[0] // 2
        arrived = exchange(keep[half:].astype(BF16), rows, stage)
        if stage:
            keep = keep[:half] + arrived.astype(F32)
    return keep[: keep.shape[0] // 2], arrived, first, (far, near, second)


def finish_kernel(keep_a, last_a, keep_b, last_b, out):
    fine = keep_a.shape[1] // 3
    for i, (keep, last) in enumerate(((keep_a, last_a), (keep_b, last_b))):
        for t in range(3):
            cols = pl.ds(t * fine, fine)
            out[:, pl.ds((2 * t + i) * fine, fine)] = keep[:, cols] + last[:, cols].astype(F32)


def branch(tokens, cell_mask, shifts, projection_in, projection_out, cotangent, *, forward):
    rows = lax.axis_size("rows")
    row_count, cols, dim = tokens.shape[1:]
    cells = row_count * cols
    half = cells // 2
    hidden = HEADS * HD
    low = 0 if forward else half
    distance = -1 if forward else 1
    core = lax.axis_index("fsdp")
    me = lax.axis_index("rows")
    blocks = 2 * rows
    m0 = jnp.asarray(slot_masks(rows, 0))
    m1 = jnp.asarray(slot_masks(rows, 1))
    mine = jnp.where(core == 0, m0, m1) ^ me
    theirs = jnp.where(core == 0, m1, m0) ^ me
    table = jnp.concatenate([core * rows + mine, (1 - core) * rows + theirs]).astype(jnp.int32)
    scal = shifts.astype(jnp.int32)
    s_row, s_col = scal[0], scal[1]
    part = lambda a: lax.slice_in_dim(a, low, low + half, axis=0)

    own = tokens.reshape(cells, dim)
    own_cot = cotangent.reshape(cells, dim)
    own_mask = cell_mask.astype(BF16).reshape(cells, 1)
    tile = 16
    mask_rows = jnp.pad(part(own_mask).T, ((0, tile - 1), (0, dim - half)))
    halo = shifted(jnp.concatenate([part(own), mask_rows, part(own_cot)], axis=0), rows, distance)
    flat_out = jnp.concatenate([projection_out[:, : dim // 2], projection_out[:, dim // 2 :]], axis=0)
    both = jnp.concatenate([projection_in, flat_out], axis=1)
    in_parts = gather_pieces(both, rows, halo)
    halo_cot = halo[half + tile :]
    halo_mask = halo[half, :half][:, None]

    cell = jnp.arange(cells, dtype=jnp.int32)
    cell_row, cell_col = cell // cols, cell % cols
    from_other = (cell_row < s_row) if forward else (cell_row >= s_row)
    pad = ((low, half - low), (0, 0))
    key_ok = jnp.where(from_other, jnp.pad(halo_mask, pad)[:, 0], own_mask[:, 0]) > 0
    at_wrap = me == (rows - 1 if forward else 0)
    region = 2 * ((cell_row < s_row) & at_wrap).astype(jnp.int32) + (cell_col < s_col).astype(
        jnp.int32
    )
    allowed = (region[:, None] == region[None, :]) & (
        key_ok[None, :] | (cell[:, None] == cell[None, :])
    )
    bias = jnp.where(allowed, 0.0, -1e30).astype(F32)

    shape_kw = dict(low=low, cols=cols, forward=forward)
    xw, normed_bf, ordered, mean, inv = call(
        functools.partial(norm_kernel, blocks=blocks, **shape_kw),
        [((cells, dim), BF16), ((cells, dim), BF16), ((dim, cells), BF16), ((cells, 1), F32), ((cells, 1), F32)],
        [SM, SM, VM, VM],
        [pltpu.VMEM((dim, cells), BF16)],
        flops=20 * cells * dim,
        moved=10 * cells * dim,
        name="norm",
    )(scal, table, own, halo)
    full_in, full_out, packed, attn, ctx, ctx_ordered = call(
        functools.partial(forward_kernel, blocks=blocks),
        [((dim, 3 * hidden), BF16), ((hidden, dim), BF16), ((cells, 3 * hidden), BF16), ((HEADS, cells, cells), F32), ((cells, hidden), BF16), ((hidden, cells), BF16)],
        [SM, SM, VM, VM] + [VM] * len(in_parts),
        [pltpu.VMEM((hidden, cells), BF16)],
        flops=6 * cells * dim * 3 * hidden,
        moved=10 << 20,
        name="fwd",
    )(table, table, normed_bf, bias, *in_parts)
    cot, keep_out, send_out = call(
        functools.partial(term_out_kernel, **shape_kw),
        [((cells, dim), BF16), ((hidden // 2, dim), F32), ((hidden // 2, dim), BF16)],
        [SM, VM, VM, VM],
        flops=2 * cells * dim * hidden,
        moved=4 << 20,
        name="term_out",
    )(scal, ctx_ordered, own_cot, halo_cot)
    swapped_out = swap_cores(send_out)
    quart = 3 * hidden // 2
    half_outs = [((cells, quart), BF16), ((dim // 2, quart), F32), ((dim // 2, quart), BF16)]
    gctx, gp_a, keep_a, send_a = call(
        backward_a_kernel,
        [((cells, hidden), BF16)] + half_outs,
        [VM] * 5,
        flops=4 * cells * dim * 3 * hidden,
        moved=6 << 20,
        name="bwd_a",
    )(cot, packed, attn, ordered, full_out)
    swapped_a = swap_cores(send_a)
    back_ctx = shifted(after(part(ctx), gp_a), rows, -distance)
    gp_b, keep_b, send_b = call(
        backward_b_kernel,
        half_outs,
        [VM, VM, VM, VM],
        flops=4 * cells * dim * 3 * hidden,
        moved=6 << 20,
        name="bwd_b",
    )(packed, attn, after(gctx, swapped_out), ordered)
    swapped_b = swap_cores(send_b)
    kept_out, last_out, _, _ = scatter_from(keep_out, swapped_out, rows)
    grad_out = kept_out + last_out.astype(F32)
    kept_a, last_a, first_a, seen_a = scatter_from(keep_a, swapped_a, rows)
    kept_b, last_b, _, _ = scatter_from(keep_b, swapped_b, rows)
    (grad_in,) = call(
        finish_kernel,
        [((dim // blocks, 3 * hidden), F32)],
        [VM] * 4,
        moved=1 << 20,
        name="finish",
    )(kept_a, last_a, kept_b, last_b)
    (grad_win,) = call(
        grad_kernel,
        [((cells, dim), BF16)],
        [VM] * 7,
        [pltpu.VMEM((cells, 3 * hidden), BF16)],
        flops=2 * cells * dim * 3 * hidden,
        moved=6 << 20,
        name="grad",
    )(xw, mean, inv, gp_a, after(gp_b, first_a), full_in, cot)
    back_grad = shifted(part(grad_win), rows, -distance)
    (output,) = call(
        functools.partial(output_kernel, **shape_kw),
        [((cells, dim), BF16)],
        [SM, VM, VM, VM, VM],
        [pltpu.VMEM((cells, hidden), BF16)],
        flops=2 * cells * dim * hidden,
        moved=3 << 20,
        name="output",
    )(scal, own, ctx, after(back_ctx, seen_a[0]), full_out)
    own_grad = jnp.where(from_other[:, None], jnp.pad(back_grad, pad), grad_win)
    shape = tokens.shape
    return (output.reshape(shape), own_grad.reshape(shape), grad_in, grad_out)


def body(tokens, cell_mask, shifts, projection_in, projection_out, cotangent):
    return lax.cond(
        shifts[0] <= tokens.shape[1] // 2,
        functools.partial(branch, forward=True),
        functools.partial(branch, forward=False),
        tokens, cell_mask, shifts, projection_in, projection_out, cotangent,
    )


def solution(mesh):
    placed = (
        P(("groups", "fsdp"), "rows", None, None),
        P(("groups", "fsdp"), "rows", None),
        P(),
        P(("fsdp", "rows"), None),
        P(("fsdp", "rows"), None),
        P(("groups", "fsdp"), "rows", None, None),
    )
    return jax.shard_map(
        body,
        mesh=mesh,
        in_specs=placed,
        out_specs=(
            P(("groups", "fsdp"), "rows", None, None),
            P(("groups", "fsdp"), "rows", None, None),
            P(("groups", "fsdp", "rows"), None),
            P(("groups", "fsdp", "rows"), None),
        ),
        check_vma=False,
    )
```

```python
import functools

import jax
import jax.numpy as jnp
import numpy as np
from jax import lax
from jax.experimental import pallas as pl
from jax.experimental.pallas import tpu as pltpu
from jax.sharding import PartitionSpec as P

HEADS = 8
HD = 64
PAIR = 2 * HD
F32 = jnp.float32
BF16 = jnp.bfloat16
VM = pl.BlockSpec(memory_space=pltpu.VMEM)
SM = pl.BlockSpec(memory_space=pltpu.SMEM)


def stage_masks(rows):
    bits = [1 << b for b in range(rows.bit_length() - 1)]
    far = bits[:1:-1]
    return (far + bits[:2], far + bits[:2][::-1])


def slot_masks(rows, core):
    masks = [0]
    for m in stage_masks(rows)[core]:
        masks = masks + [a ^ m for a in masks]
    return np.array(masks, np.int32)


def exchange(block, rows, stage):
    masks = stage_masks(rows)
    pairs = [
        (c * rows + i, c * rows + (i ^ masks[c][stage])) for c in range(2) for i in range(rows)
    ]
    return lax.ppermute(block, ("fsdp", "rows"), pairs)


def swap_cores(block):
    return lax.ppermute(block, "fsdp", [(0, 1), (1, 0)])


def shifted(block, rows, distance):
    return lax.ppermute(block, "rows", [((i - distance) % rows, i) for i in range(rows)])


def call(kernel, outs, specs, scratch=(), flops=0, moved=0, name=None):
    return pl.pallas_call(
        kernel,
        out_shape=tuple(jax.ShapeDtypeStruct(s, d) for s, d in outs),
        in_specs=list(specs),
        out_specs=tuple(VM for _ in outs),
        scratch_shapes=list(scratch),
        compiler_params=pltpu.CompilerParams(vmem_limit_bytes=40 << 20),
        cost_estimate=pl.CostEstimate(flops=flops, bytes_accessed=moved, transcendentals=0),
        name=name,
    )


def dot(a, b, ca=1, cb=0):
    return lax.dot_general(a, b, (((ca,), (cb,)), ((), ())), preferred_element_type=F32)


def place(full_in, full_out, piece, table, first, count):
    size = piece.shape[0] // count
    small = size // 2
    wide = full_in.shape[1]
    side = full_out.shape[1] // 2

    def step(j, carry):
        block = table[first + j]
        at = pl.multiple_of(block * size, size)
        at_out = pl.multiple_of(block * small, small)
        of = pl.multiple_of(j * size, size)
        full_in[pl.ds(at, size), :] = piece[pl.ds(of, size), pl.ds(0, wide)]
        for h in range(2):
            from_at = pl.multiple_of(of + h * small, small)
            full_out[pl.ds(at_out, small), pl.ds(h * side, side)] = piece[
                pl.ds(from_at, small), pl.ds(wide, side)
            ]
        return carry

    lax.fori_loop(0, count, step, 0)


def pick(dst, src, table, count, size):
    def step(j, carry):
        at = pl.multiple_of(table[j] * size, size)
        dst[pl.ds(pl.multiple_of(j * size, size), size), :] = src[pl.ds(at, size), :]
        return carry

    lax.fori_loop(0, count, step, 0)


def borrowed_rows(scal, low, count, cols, forward):
    row = (lax.broadcasted_iota(jnp.int32, (count, 1), 0) + low) // cols
    return row < scal[0] if forward else row >= scal[0]


def norm_kernel(scal, table, own, halo, xw, normed_bf, ordered, mean_out, inv_out, turned, *, low, cols, forward, blocks):
    half = own.shape[0] // 2
    take = borrowed_rows(scal, low, half, cols, forward)
    keep_low = half - low
    xw[pl.ds(keep_low, half), :] = own[pl.ds(keep_low, half), :]
    mixed = jnp.where(take, halo[pl.ds(0, half), :].astype(F32), own[pl.ds(low, half), :].astype(F32))
    xw[pl.ds(low, half), :] = mixed.astype(BF16)
    x = xw[...].astype(F32)
    mean = jnp.mean(x, axis=-1, keepdims=True)
    centered = x - mean
    inv = lax.rsqrt(jnp.mean(centered * centered, axis=-1, keepdims=True) + 1e-05)
    normed = centered * inv
    normed_bf[...] = normed.astype(BF16)
    mean_out[...] = mean
    inv_out[...] = inv
    turned[...] = normed.T.astype(BF16)
    pick(ordered, turned, table, blocks, turned.shape[0] // blocks)


def forward_kernel(place_at, order, normed_bf, bias, *refs, blocks):
    pieces, (full, full_out, packed, attn, ctx, ctx_ordered, turned) = refs[:-7], refs[-7:]
    each = blocks // len(pieces)
    for i, w in enumerate(pieces):
        place(full, full_out, w, place_at, i * each, each)
    hidden = ctx.shape[1]
    packed[...] = dot(normed_bf[...], full[...]).astype(BF16)
    cells = normed_bf.shape[0]
    first = lax.broadcasted_iota(jnp.int32, (cells, PAIR), 1) < HD
    for p in range(HEADS // 2):
        lanes = pl.ds(p * PAIR, PAIR)
        q = packed[:, lanes].astype(F32)
        k = packed[:, pl.ds(hidden + p * PAIR, PAIR)]
        v = packed[:, pl.ds(2 * hidden + p * PAIR, PAIR)]
        parts = []
        for side in range(2):
            q_one = jnp.where(first if side == 0 else ~first, q, 0.0).astype(BF16)
            scores = dot(q_one, k, 1, 1) * (HD ** (-0.5)) + bias[...]
            e = jnp.exp(scores - jnp.max(scores, axis=-1, keepdims=True))
            a = e * (1.0 / jnp.sum(e, axis=-1, keepdims=True))
            attn[2 * p + side] = a
            parts.append(dot(a.astype(BF16), v))
        both = jnp.where(first, parts[0], parts[1])
        ctx[:, lanes] = both.astype(BF16)
        turned[lanes, :] = both.T.astype(BF16)
    pick(ctx_ordered, turned, order, blocks, turned.shape[0] // blocks)


def term_out_kernel(scal, ctx_ordered, own, halo, cot, keep, send, *, low, cols, forward):
    half = halo.shape[0]
    take = borrowed_rows(scal, low, half, cols, forward)
    keep_low = half - low
    cot[pl.ds(keep_low, half), :] = own[pl.ds(keep_low, half), :]
    cot[pl.ds(low, half), :] = jnp.where(
        take, halo[...].astype(F32), own[pl.ds(low, half), :].astype(F32)
    ).astype(BF16)
    n = keep.shape[0]
    send[...] = dot(ctx_ordered[pl.ds(n, n), :], cot[...]).astype(BF16)
    keep[...] = dot(ctx_ordered[pl.ds(0, n), :], cot[...])


def half_backward(packed, attn, gctx, gp, first_pair, pairs):
    cells = packed.shape[0]
    hidden = packed.shape[1] // 3
    width = pairs * PAIR
    first = lax.broadcasted_iota(jnp.int32, (cells, PAIR), 1) < HD
    for i in range(pairs):
        p = first_pair + i
        q = packed[:, pl.ds(p * PAIR, PAIR)]
        k = packed[:, pl.ds(hidden + p * PAIR, PAIR)]
        v = packed[:, pl.ds(2 * hidden + p * PAIR, PAIR)]
        g = gctx[:, pl.ds(p * PAIR, PAIR)]
        gf = g.astype(F32)
        gq, gk, gv = [], [], []
        for side in range(2):
            g_one = jnp.where(first if side == 0 else ~first, gf, 0.0).astype(BF16)
            a = attn[2 * p + side]
            ga = dot(g_one, v, 1, 1)
            inner = jnp.sum(ga * a, axis=-1, keepdims=True)
            gs = (a * (ga - inner) * (HD ** (-0.5))).astype(BF16)
            gq.append(dot(gs, k))
            gk.append(dot(gs, q, 0, 0))
            gv.append(dot(a.astype(BF16), g, 0, 0))
        for t, two in enumerate((gq, gk, gv)):
            gp[:, pl.ds(t * width + i * PAIR, PAIR)] = jnp.where(first, two[0], two[1]).astype(BF16)


def term_of(ordered, gp, keep, send):
    n = keep.shape[0]
    send[...] = dot(ordered[pl.ds(n, n), :], gp[...]).astype(BF16)
    keep[...] = dot(ordered[pl.ds(0, n), :], gp[...])


def backward_a_kernel(cot, packed, attn, ordered, full, gctx, gp, keep, send):
    gctx[...] = dot(cot[...], full[...], 1, 1).astype(BF16)
    half_backward(packed, attn, gctx, gp, 0, HEADS // 4)
    term_of(ordered, gp, keep, send)


def backward_b_kernel(packed, attn, gctx, ordered, gp, keep, send):
    half_backward(packed, attn, gctx, gp, HEADS // 4, HEADS // 4)
    term_of(ordered, gp, keep, send)


def grad_kernel(xw, mean, inv, gp_a, gp_b, full, cot, grad, gp):
    width = gp.shape[1] // 6
    for t in range(3):
        gp[:, pl.ds(2 * t * width, width)] = gp_a[:, pl.ds(t * width, width)]
        gp[:, pl.ds((2 * t + 1) * width, width)] = gp_b[:, pl.ds(t * width, width)]
    gn = dot(gp[...], full[...], 1, 1)
    normed = (xw[...].astype(F32) - mean[...]) * inv[...]
    m1 = jnp.mean(gn, axis=-1, keepdims=True)
    m2 = jnp.mean(gn * normed, axis=-1, keepdims=True)
    grad[...] = (cot[...].astype(F32) + inv[...] * (gn - m1 - normed * m2)).astype(BF16)


def output_kernel(scal, own, ctx, back, full, out, mixed, *, low, cols, forward):
    half = back.shape[0]
    take = borrowed_rows(scal, low, half, cols, forward)
    keep_low = half - low
    mixed[pl.ds(keep_low, half), :] = ctx[pl.ds(keep_low, half), :]
    mixed[pl.ds(low, half), :] = jnp.where(
        take, back[...].astype(F32), ctx[pl.ds(low, half), :].astype(F32)
    ).astype(BF16)
    out[...] = (own[...].astype(F32) + dot(mixed[...], full[...])).astype(BF16)


def after(value, *done):
    return lax.optimization_barrier((value, *done))[0]


def gather_pieces(shard, rows, halo):
    stages = len(stage_masks(rows)[0])
    own = shard
    for stage in range(stages - 3):
        own = jnp.concatenate([own, exchange(own, rows, stage)], axis=0)
    a, b, c = stages - 3, stages - 2, stages - 1
    got_a = exchange(own, rows, a)
    got_b = exchange(own, rows, b)
    got_c = exchange(own, rows, c)
    got_ab = exchange(after(got_a, got_b), rows, b)
    got_ac = exchange(after(got_a, got_c), rows, c)
    got_bc = exchange(after(got_b, got_c), rows, c)
    got_abc = exchange(after(got_ab, got_ac, halo), rows, c)
    held = (own, got_a, got_b, got_ab, got_c, got_ac, got_bc, got_abc)
    return held + tuple(swap_cores(x) for x in held)


def scatter_from(keep, arrived, rows):
    n = len(stage_masks(rows)[0])
    q = keep.shape[0] // 4
    keep = keep + arrived.astype(F32)
    first = keep[2 * q :].astype(BF16)
    h = 2 * q
    far = exchange(keep[h:].astype(BF16), rows, n - 1)
    keep = keep[:h] + far.astype(F32)
    near = second = exchange(keep[q:].astype(BF16), rows, n - 2)
    keep = keep[:q] + second.astype(F32)
    for stage in range(n - 3, -1, -1):
        half = keep.shape[0] // 2
        arrived = exchange(keep[half:].astype(BF16), rows, stage)
        if stage:
            keep = keep[:half] + arrived.astype(F32)
    return keep[: keep.shape[0] // 2], arrived, first, (far, near, second)


def finish_kernel(keep_a, last_a, keep_b, last_b, out):
    fine = keep_a.shape[1] // 3
    for i, (keep, last) in enumerate(((keep_a, last_a), (keep_b, last_b))):
        for t in range(3):
            cols = pl.ds(t * fine, fine)
            out[:, pl.ds((2 * t + i) * fine, fine)] = keep[:, cols] + last[:, cols].astype(F32)


def branch(tokens, cell_mask, shifts, projection_in, projection_out, cotangent, *, forward):
    rows = lax.axis_size("rows")
    row_count, cols, dim = tokens.shape[1:]
    cells = row_count * cols
    half = cells // 2
    hidden = HEADS * HD
    low = 0 if forward else half
    distance = -1 if forward else 1
    core = lax.axis_index("fsdp")
    me = lax.axis_index("rows")
    blocks = 2 * rows
    m0 = jnp.asarray(slot_masks(rows, 0))
    m1 = jnp.asarray(slot_masks(rows, 1))
    mine = jnp.where(core == 0, m0, m1) ^ me
    theirs = jnp.where(core == 0, m1, m0) ^ me
    table = jnp.concatenate([core * rows + mine, (1 - core) * rows + theirs]).astype(jnp.int32)
    scal = shifts.astype(jnp.int32)
    s_row, s_col = scal[0], scal[1]
    part = lambda a: lax.slice_in_dim(a, low, low + half, axis=0)

    own = tokens.reshape(cells, dim)
    own_cot = cotangent.reshape(cells, dim)
    own_mask = cell_mask.astype(BF16).reshape(cells, 1)
    tile = 16
    mask_rows = jnp.pad(part(own_mask).T, ((0, tile - 1), (0, dim - half)))
    halo = shifted(jnp.concatenate([part(own), mask_rows, part(own_cot)], axis=0), rows, distance)
    flat_out = jnp.concatenate([projection_out[:, : dim // 2], projection_out[:, dim // 2 :]], axis=0)
    both = jnp.concatenate([projection_in, flat_out], axis=1)
    in_parts = gather_pieces(both, rows, halo)
    halo_cot = halo[half + tile :]
    halo_mask = halo[half, :half][:, None]

    cell = jnp.arange(cells, dtype=jnp.int32)
    cell_row, cell_col = cell // cols, cell % cols
    from_other = (cell_row < s_row) if forward else (cell_row >= s_row)
    pad = ((low, half - low), (0, 0))
    key_ok = jnp.where(from_other, jnp.pad(halo_mask, pad)[:, 0], own_mask[:, 0]) > 0
    at_wrap = me == (rows - 1 if forward else 0)
    region = 2 * ((cell_row < s_row) & at_wrap).astype(jnp.int32) + (cell_col < s_col).astype(
        jnp.int32
    )
    allowed = (region[:, None] == region[None, :]) & (
        key_ok[None, :] | (cell[:, None] == cell[None, :])
    )
    bias = jnp.where(allowed, 0.0, -1e30).astype(F32)

    shape_kw = dict(low=low, cols=cols, forward=forward)
    xw, normed_bf, ordered, mean, inv = call(
        functools.partial(norm_kernel, blocks=blocks, **shape_kw),
        [((cells, dim), BF16), ((cells, dim), BF16), ((dim, cells), BF16), ((cells, 1), F32), ((cells, 1), F32)],
        [SM, SM, VM, VM],
        [pltpu.VMEM((dim, cells), BF16)],
        flops=20 * cells * dim,
        moved=10 * cells * dim,
        name="norm",
    )(scal, table, own, halo)
    full_in, full_out, packed, attn, ctx, ctx_ordered = call(
        functools.partial(forward_kernel, blocks=blocks),
        [((dim, 3 * hidden), BF16), ((hidden, dim), BF16), ((cells, 3 * hidden), BF16), ((HEADS, cells, cells), F32), ((cells, hidden), BF16), ((hidden, cells), BF16)],
        [SM, SM, VM, VM] + [VM] * len(in_parts),
        [pltpu.VMEM((hidden, cells), BF16)],
        flops=6 * cells * dim * 3 * hidden,
        moved=10 << 20,
        name="fwd",
    )(table, table, normed_bf, bias, *in_parts)
    cot, keep_out, send_out = call(
        functools.partial(term_out_kernel, **shape_kw),
        [((cells, dim), BF16), ((hidden // 2, dim), F32), ((hidden // 2, dim), BF16)],
        [SM, VM, VM, VM],
        flops=2 * cells * dim * hidden,
        moved=4 << 20,
        name="term_out",
    )(scal, ctx_ordered, own_cot, halo_cot)
    swapped_out = swap_cores(send_out)
    quart = 3 * hidden // 2
    half_outs = [((cells, quart), BF16), ((dim // 2, quart), F32), ((dim // 2, quart), BF16)]
    gctx, gp_a, keep_a, send_a = call(
        backward_a_kernel,
        [((cells, hidden), BF16)] + half_outs,
        [VM] * 5,
        flops=4 * cells * dim * 3 * hidden,
        moved=6 << 20,
        name="bwd_a",
    )(cot, packed, attn, ordered, full_out)
    swapped_a = swap_cores(send_a)
    back_ctx = shifted(after(part(ctx), gp_a), rows, -distance)
    gp_b, keep_b, send_b = call(
        backward_b_kernel,
        half_outs,
        [VM, VM, VM, VM],
        flops=4 * cells * dim * 3 * hidden,
        moved=6 << 20,
        name="bwd_b",
    )(packed, attn, after(gctx, swapped_out), ordered)
    swapped_b = swap_cores(send_b)
    kept_out, last_out, _, _ = scatter_from(keep_out, swapped_out, rows)
    grad_out = kept_out + last_out.astype(F32)
    kept_a, last_a, first_a, seen_a = scatter_from(keep_a, swapped_a, rows)
    kept_b, last_b, _, seen_b = scatter_from(keep_b, swapped_b, rows)
    (grad_in,) = call(
        finish_kernel,
        [((dim // blocks, 3 * hidden), F32)],
        [VM] * 4,
        moved=1 << 20,
        name="finish",
    )(kept_a, last_a, kept_b, last_b)
    (grad_win,) = call(
        grad_kernel,
        [((cells, dim), BF16)],
        [VM] * 7,
        [pltpu.VMEM((cells, 3 * hidden), BF16)],
        flops=2 * cells * dim * 3 * hidden,
        moved=6 << 20,
        name="grad",
    )(xw, mean, inv, gp_a, after(gp_b, first_a, back_ctx), full_in, cot)
    back_grad = shifted(after(part(grad_win), seen_b[0]), rows, -distance)
    (output,) = call(
        functools.partial(output_kernel, **shape_kw),
        [((cells, dim), BF16)],
        [SM, VM, VM, VM, VM],
        [pltpu.VMEM((cells, hidden), BF16)],
        flops=2 * cells * dim * hidden,
        moved=3 << 20,
        name="output",
    )(scal, own, ctx, after(back_ctx, seen_a[0]), full_out)
    own_grad = jnp.where(from_other[:, None], jnp.pad(back_grad, pad), grad_win)
    shape = tokens.shape
    return (output.reshape(shape), own_grad.reshape(shape), grad_in, grad_out)


def body(tokens, cell_mask, shifts, projection_in, projection_out, cotangent):
    return lax.cond(
        shifts[0] <= tokens.shape[1] // 2,
        functools.partial(branch, forward=True),
        functools.partial(branch, forward=False),
        tokens, cell_mask, shifts, projection_in, projection_out, cotangent,
    )


def solution(mesh):
    placed = (
        P(("groups", "fsdp"), "rows", None, None),
        P(("groups", "fsdp"), "rows", None),
        P(),
        P(("fsdp", "rows"), None),
        P(("fsdp", "rows"), None),
        P(("groups", "fsdp"), "rows", None, None),
    )
    return jax.shard_map(
        body,
        mesh=mesh,
        in_specs=placed,
        out_specs=(
            P(("groups", "fsdp"), "rows", None, None),
            P(("groups", "fsdp"), "rows", None, None),
            P(("groups", "fsdp", "rows"), None),
            P(("groups", "fsdp", "rows"), None),
        ),
        check_vma=False,
    )
```

```python
import functools

import jax
import jax.numpy as jnp
import numpy as np
from jax import lax
from jax.experimental import pallas as pl
from jax.experimental.pallas import tpu as pltpu
from jax.sharding import PartitionSpec as P

HEADS = 8
HD = 64
PAIR = 2 * HD
F32 = jnp.float32
BF16 = jnp.bfloat16
VM = pl.BlockSpec(memory_space=pltpu.VMEM)
SM = pl.BlockSpec(memory_space=pltpu.SMEM)


def stage_masks(rows):
    bits = [1 << b for b in range(rows.bit_length() - 1)]
    far = bits[:1:-1]
    return (far + bits[:2], far + bits[:2][::-1])


def slot_masks(rows, core):
    masks = [0]
    for m in stage_masks(rows)[core]:
        masks = masks + [a ^ m for a in masks]
    return np.array(masks, np.int32)


def exchange(block, rows, stage):
    masks = stage_masks(rows)
    pairs = [
        (c * rows + i, c * rows + (i ^ masks[c][stage])) for c in range(2) for i in range(rows)
    ]
    return lax.ppermute(block, ("fsdp", "rows"), pairs)


def swap_cores(block):
    return lax.ppermute(block, "fsdp", [(0, 1), (1, 0)])


def shifted(block, rows, distance):
    return lax.ppermute(block, "rows", [((i - distance) % rows, i) for i in range(rows)])


def call(kernel, outs, specs, scratch=(), flops=0, moved=0, name=None):
    return pl.pallas_call(
        kernel,
        out_shape=tuple(jax.ShapeDtypeStruct(s, d) for s, d in outs),
        in_specs=list(specs),
        out_specs=tuple(VM for _ in outs),
        scratch_shapes=list(scratch),
        compiler_params=pltpu.CompilerParams(vmem_limit_bytes=40 << 20),
        cost_estimate=pl.CostEstimate(flops=flops, bytes_accessed=moved, transcendentals=0),
        name=name,
    )


def dot(a, b, ca=1, cb=0):
    return lax.dot_general(a, b, (((ca,), (cb,)), ((), ())), preferred_element_type=F32)


def place(full_in, full_out, piece, table, first, count):
    size = piece.shape[0] // count
    small = size // 2
    wide = full_in.shape[1]
    side = full_out.shape[1] // 2

    def step(j, carry):
        block = table[first + j]
        at = pl.multiple_of(block * size, size)
        at_out = pl.multiple_of(block * small, small)
        of = pl.multiple_of(j * size, size)
        full_in[pl.ds(at, size), :] = piece[pl.ds(of, size), pl.ds(0, wide)]
        for h in range(2):
            from_at = pl.multiple_of(of + h * small, small)
            full_out[pl.ds(at_out, small), pl.ds(h * side, side)] = piece[
                pl.ds(from_at, small), pl.ds(wide, side)
            ]
        return carry

    lax.fori_loop(0, count, step, 0)


def pick(dst, src, table, count, size):
    def step(j, carry):
        at = pl.multiple_of(table[j] * size, size)
        dst[pl.ds(pl.multiple_of(j * size, size), size), :] = src[pl.ds(at, size), :]
        return carry

    lax.fori_loop(0, count, step, 0)


def borrowed_rows(scal, low, count, cols, forward):
    row = (lax.broadcasted_iota(jnp.int32, (count, 1), 0) + low) // cols
    return row < scal[0] if forward else row >= scal[0]


def norm_kernel(scal, table, own, halo, xw, normed_bf, ordered, mean_out, inv_out, turned, *, low, cols, forward, blocks):
    half = own.shape[0] // 2
    take = borrowed_rows(scal, low, half, cols, forward)
    keep_low = half - low
    xw[pl.ds(keep_low, half), :] = own[pl.ds(keep_low, half), :]
    mixed = jnp.where(take, halo[pl.ds(0, half), :].astype(F32), own[pl.ds(low, half), :].astype(F32))
    xw[pl.ds(low, half), :] = mixed.astype(BF16)
    x = xw[...].astype(F32)
    mean = jnp.mean(x, axis=-1, keepdims=True)
    centered = x - mean
    inv = lax.rsqrt(jnp.mean(centered * centered, axis=-1, keepdims=True) + 1e-05)
    normed = centered * inv
    normed_bf[...] = normed.astype(BF16)
    mean_out[...] = mean
    inv_out[...] = inv
    turned[...] = normed.T.astype(BF16)
    pick(ordered, turned, table, blocks, turned.shape[0] // blocks)


def forward_kernel(place_at, order, normed_bf, bias, *refs, blocks):
    pieces, (full, full_out, packed, attn, ctx, ctx_ordered, turned) = refs[:-7], refs[-7:]
    each = blocks // len(pieces)
    for i, w in enumerate(pieces):
        place(full, full_out, w, place_at, i * each, each)
    hidden = ctx.shape[1]
    packed[...] = dot(normed_bf[...], full[...]).astype(BF16)
    cells = normed_bf.shape[0]
    first = lax.broadcasted_iota(jnp.int32, (cells, PAIR), 1) < HD
    for p in range(HEADS // 2):
        lanes = pl.ds(p * PAIR, PAIR)
        q = packed[:, lanes].astype(F32)
        k = packed[:, pl.ds(hidden + p * PAIR, PAIR)]
        v = packed[:, pl.ds(2 * hidden + p * PAIR, PAIR)]
        parts = []
        for side in range(2):
            q_one = jnp.where(first if side == 0 else ~first, q, 0.0).astype(BF16)
            scores = dot(q_one, k, 1, 1) * (HD ** (-0.5)) + bias[...]
            e = jnp.exp(scores - jnp.max(scores, axis=-1, keepdims=True))
            a = e * (1.0 / jnp.sum(e, axis=-1, keepdims=True))
            attn[2 * p + side] = a
            parts.append(dot(a.astype(BF16), v))
        both = jnp.where(first, parts[0], parts[1])
        ctx[:, lanes] = both.astype(BF16)
        turned[lanes, :] = both.T.astype(BF16)
    pick(ctx_ordered, turned, order, blocks, turned.shape[0] // blocks)


def term_out_kernel(scal, ctx_ordered, own, halo, cot, keep, send, *, low, cols, forward):
    half = halo.shape[0]
    take = borrowed_rows(scal, low, half, cols, forward)
    keep_low = half - low
    cot[pl.ds(keep_low, half), :] = own[pl.ds(keep_low, half), :]
    cot[pl.ds(low, half), :] = jnp.where(
        take, halo[...].astype(F32), own[pl.ds(low, half), :].astype(F32)
    ).astype(BF16)
    n = keep.shape[0]
    send[...] = dot(ctx_ordered[pl.ds(n, n), :], cot[...]).astype(BF16)
    keep[...] = dot(ctx_ordered[pl.ds(0, n), :], cot[...])


def half_backward(packed, attn, gctx, gp, first_pair, pairs):
    cells = packed.shape[0]
    hidden = packed.shape[1] // 3
    width = pairs * PAIR
    first = lax.broadcasted_iota(jnp.int32, (cells, PAIR), 1) < HD
    for i in range(pairs):
        p = first_pair + i
        q = packed[:, pl.ds(p * PAIR, PAIR)]
        k = packed[:, pl.ds(hidden + p * PAIR, PAIR)]
        v = packed[:, pl.ds(2 * hidden + p * PAIR, PAIR)]
        g = gctx[:, pl.ds(p * PAIR, PAIR)]
        gf = g.astype(F32)
        gq, gk, gv = [], [], []
        for side in range(2):
            g_one = jnp.where(first if side == 0 else ~first, gf, 0.0).astype(BF16)
            a = attn[2 * p + side]
            ga = dot(g_one, v, 1, 1)
            inner = jnp.sum(ga * a, axis=-1, keepdims=True)
            gs = (a * (ga - inner) * (HD ** (-0.5))).astype(BF16)
            gq.append(dot(gs, k))
            gk.append(dot(gs, q, 0, 0))
            gv.append(dot(a.astype(BF16), g, 0, 0))
        for t, two in enumerate((gq, gk, gv)):
            gp[:, pl.ds(t * width + i * PAIR, PAIR)] = jnp.where(first, two[0], two[1]).astype(BF16)


def term_of(ordered, gp, keep, send):
    n = keep.shape[0]
    send[...] = dot(ordered[pl.ds(n, n), :], gp[...]).astype(BF16)
    keep[...] = dot(ordered[pl.ds(0, n), :], gp[...])


def backward_a_kernel(cot, packed, attn, ordered, full, gctx, gp, keep, send):
    gctx[...] = dot(cot[...], full[...], 1, 1).astype(BF16)
    half_backward(packed, attn, gctx, gp, 0, HEADS // 4)
    term_of(ordered, gp, keep, send)


def backward_b_kernel(packed, attn, gctx, ordered, gp, keep, send):
    half_backward(packed, attn, gctx, gp, HEADS // 4, HEADS // 4)
    term_of(ordered, gp, keep, send)


def grad_kernel(xw, mean, inv, gp_a, gp_b, full, cot, grad, gp):
    width = gp.shape[1] // 6
    for t in range(3):
        gp[:, pl.ds(2 * t * width, width)] = gp_a[:, pl.ds(t * width, width)]
        gp[:, pl.ds((2 * t + 1) * width, width)] = gp_b[:, pl.ds(t * width, width)]
    gn = dot(gp[...], full[...], 1, 1)
    normed = (xw[...].astype(F32) - mean[...]) * inv[...]
    m1 = jnp.mean(gn, axis=-1, keepdims=True)
    m2 = jnp.mean(gn * normed, axis=-1, keepdims=True)
    grad[...] = (cot[...].astype(F32) + inv[...] * (gn - m1 - normed * m2)).astype(BF16)


def output_kernel(scal, own, ctx, back, full, out, mixed, *, low, cols, forward):
    half = back.shape[0]
    take = borrowed_rows(scal, low, half, cols, forward)
    keep_low = half - low
    mixed[pl.ds(keep_low, half), :] = ctx[pl.ds(keep_low, half), :]
    mixed[pl.ds(low, half), :] = jnp.where(
        take, back[...].astype(F32), ctx[pl.ds(low, half), :].astype(F32)
    ).astype(BF16)
    out[...] = (own[...].astype(F32) + dot(mixed[...], full[...])).astype(BF16)


def after(value, *done):
    return lax.optimization_barrier((value, *done))[0]


def gather_pieces(shard, rows, halo):
    stages = len(stage_masks(rows)[0])
    own = shard
    for stage in range(stages - 3):
        own = jnp.concatenate([own, exchange(own, rows, stage)], axis=0)
    a, b, c = stages - 3, stages - 2, stages - 1
    got_a = exchange(own, rows, a)
    got_b = exchange(own, rows, b)
    got_c = exchange(own, rows, c)
    got_ab = exchange(after(got_a, got_b), rows, b)
    got_ac = exchange(after(got_a, got_c), rows, c)
    got_bc = exchange(after(got_b, got_c), rows, c)
    got_abc = exchange(after(got_ab, got_ac, halo), rows, c)
    held = (own, got_a, got_b, got_ab, got_c, got_ac, got_bc, got_abc)
    return held + tuple(swap_cores(x) for x in held)


def scatter_from(keep, arrived, rows):
    n = len(stage_masks(rows)[0])
    q = keep.shape[0] // 4
    keep = keep + arrived.astype(F32)
    first = keep[2 * q :].astype(BF16)
    h = 2 * q
    far = exchange(keep[h:].astype(BF16), rows, n - 1)
    keep = keep[:h] + far.astype(F32)
    near = second = exchange(keep[q:].astype(BF16), rows, n - 2)
    keep = keep[:q] + second.astype(F32)
    for stage in range(n - 3, -1, -1):
        half = keep.shape[0] // 2
        arrived = exchange(keep[half:].astype(BF16), rows, stage)
        if stage:
            keep = keep[:half] + arrived.astype(F32)
    return keep[: keep.shape[0] // 2], arrived, first, (far, near, second)


def finish_kernel(keep_a, last_a, keep_b, last_b, out):
    fine = keep_a.shape[1] // 3
    for i, (keep, last) in enumerate(((keep_a, last_a), (keep_b, last_b))):
        for t in range(3):
            cols = pl.ds(t * fine, fine)
            out[:, pl.ds((2 * t + i) * fine, fine)] = keep[:, cols] + last[:, cols].astype(F32)


def branch(tokens, cell_mask, shifts, projection_in, projection_out, cotangent, *, forward):
    rows = lax.axis_size("rows")
    row_count, cols, dim = tokens.shape[1:]
    cells = row_count * cols
    half = cells // 2
    hidden = HEADS * HD
    low = 0 if forward else half
    distance = -1 if forward else 1
    core = lax.axis_index("fsdp")
    me = lax.axis_index("rows")
    blocks = 2 * rows
    m0 = jnp.asarray(slot_masks(rows, 0))
    m1 = jnp.asarray(slot_masks(rows, 1))
    mine = jnp.where(core == 0, m0, m1) ^ me
    theirs = jnp.where(core == 0, m1, m0) ^ me
    table = jnp.concatenate([core * rows + mine, (1 - core) * rows + theirs]).astype(jnp.int32)
    scal = shifts.astype(jnp.int32)
    s_row, s_col = scal[0], scal[1]
    part = lambda a: lax.slice_in_dim(a, low, low + half, axis=0)

    own = tokens.reshape(cells, dim)
    own_cot = cotangent.reshape(cells, dim)
    own_mask = cell_mask.astype(BF16).reshape(cells, 1)
    tile = 16
    mask_rows = jnp.pad(part(own_mask).T, ((0, tile - 1), (0, dim - half)))
    halo = shifted(jnp.concatenate([part(own), mask_rows, part(own_cot)], axis=0), rows, distance)
    flat_out = jnp.concatenate([projection_out[:, : dim // 2], projection_out[:, dim // 2 :]], axis=0)
    both = jnp.concatenate([projection_in, flat_out], axis=1)
    in_parts = gather_pieces(both, rows, halo)
    halo_cot = halo[half + tile :]
    halo_mask = halo[half, :half][:, None]

    cell = jnp.arange(cells, dtype=jnp.int32)
    cell_row, cell_col = cell // cols, cell % cols
    from_other = (cell_row < s_row) if forward else (cell_row >= s_row)
    pad = ((low, half - low), (0, 0))
    key_ok = jnp.where(from_other, jnp.pad(halo_mask, pad)[:, 0], own_mask[:, 0]) > 0
    at_wrap = me == (rows - 1 if forward else 0)
    region = 2 * ((cell_row < s_row) & at_wrap).astype(jnp.int32) + (cell_col < s_col).astype(
        jnp.int32
    )
    allowed = (region[:, None] == region[None, :]) & (
        key_ok[None, :] | (cell[:, None] == cell[None, :])
    )
    bias = jnp.where(allowed, 0.0, -1e30).astype(F32)

    shape_kw = dict(low=low, cols=cols, forward=forward)
    xw, normed_bf, ordered, mean, inv = call(
        functools.partial(norm_kernel, blocks=blocks, **shape_kw),
        [((cells, dim), BF16), ((cells, dim), BF16), ((dim, cells), BF16), ((cells, 1), F32), ((cells, 1), F32)],
        [SM, SM, VM, VM],
        [pltpu.VMEM((dim, cells), BF16)],
        flops=20 * cells * dim,
        moved=10 * cells * dim,
        name="norm",
    )(scal, table, own, halo)
    full_in, full_out, packed, attn, ctx, ctx_ordered = call(
        functools.partial(forward_kernel, blocks=blocks),
        [((dim, 3 * hidden), BF16), ((hidden, dim), BF16), ((cells, 3 * hidden), BF16), ((HEADS, cells, cells), F32), ((cells, hidden), BF16), ((hidden, cells), BF16)],
        [SM, SM, VM, VM] + [VM] * len(in_parts),
        [pltpu.VMEM((hidden, cells), BF16)],
        flops=6 * cells * dim * 3 * hidden,
        moved=10 << 20,
        name="fwd",
    )(table, table, normed_bf, bias, *in_parts)
    cot, keep_out, send_out = call(
        functools.partial(term_out_kernel, **shape_kw),
        [((cells, dim), BF16), ((hidden // 2, dim), F32), ((hidden // 2, dim), BF16)],
        [SM, VM, VM, VM],
        flops=2 * cells * dim * hidden,
        moved=4 << 20,
        name="term_out",
    )(scal, ctx_ordered, own_cot, halo_cot)
    swapped_out = swap_cores(send_out)
    quart = 3 * hidden // 2
    half_outs = [((cells, quart), BF16), ((dim // 2, quart), F32), ((dim // 2, quart), BF16)]
    gctx, gp_a, keep_a, send_a = call(
        backward_a_kernel,
        [((cells, hidden), BF16)] + half_outs,
        [VM] * 5,
        flops=4 * cells * dim * 3 * hidden,
        moved=6 << 20,
        name="bwd_a",
    )(cot, packed, attn, ordered, full_out)
    swapped_a = swap_cores(send_a)
    back_ctx = shifted(after(part(ctx), gp_a), rows, -distance)
    gp_b, keep_b, send_b = call(
        backward_b_kernel,
        half_outs,
        [VM, VM, VM, VM],
        flops=4 * cells * dim * 3 * hidden,
        moved=6 << 20,
        name="bwd_b",
    )(packed, attn, after(gctx, swapped_out), ordered)
    swapped_b = swap_cores(after(send_b, swapped_a))
    kept_out, last_out, _, _ = scatter_from(keep_out, swapped_out, rows)
    grad_out = kept_out + last_out.astype(F32)
    kept_a, last_a, first_a, seen_a = scatter_from(keep_a, swapped_a, rows)
    kept_b, last_b, _, seen_b = scatter_from(keep_b, swapped_b, rows)
    (grad_in,) = call(
        finish_kernel,
        [((dim // blocks, 3 * hidden), F32)],
        [VM] * 4,
        moved=1 << 20,
        name="finish",
    )(kept_a, last_a, kept_b, last_b)
    (grad_win,) = call(
        grad_kernel,
        [((cells, dim), BF16)],
        [VM] * 7,
        [pltpu.VMEM((cells, 3 * hidden), BF16)],
        flops=2 * cells * dim * 3 * hidden,
        moved=6 << 20,
        name="grad",
    )(xw, mean, inv, gp_a, after(gp_b, first_a, back_ctx), full_in, cot)
    back_grad = shifted(after(part(grad_win), seen_b[0]), rows, -distance)
    (output,) = call(
        functools.partial(output_kernel, **shape_kw),
        [((cells, dim), BF16)],
        [SM, VM, VM, VM, VM],
        [pltpu.VMEM((cells, hidden), BF16)],
        flops=2 * cells * dim * hidden,
        moved=3 << 20,
        name="output",
    )(scal, own, ctx, after(back_ctx, seen_a[0]), full_out)
    own_grad = jnp.where(from_other[:, None], jnp.pad(back_grad, pad), grad_win)
    shape = tokens.shape
    return (output.reshape(shape), own_grad.reshape(shape), grad_in, grad_out)


def body(tokens, cell_mask, shifts, projection_in, projection_out, cotangent):
    return lax.cond(
        shifts[0] <= tokens.shape[1] // 2,
        functools.partial(branch, forward=True),
        functools.partial(branch, forward=False),
        tokens, cell_mask, shifts, projection_in, projection_out, cotangent,
    )


def solution(mesh):
    placed = (
        P(("groups", "fsdp"), "rows", None, None),
        P(("groups", "fsdp"), "rows", None),
        P(),
        P(("fsdp", "rows"), None),
        P(("fsdp", "rows"), None),
        P(("groups", "fsdp"), "rows", None, None),
    )
    return jax.shard_map(
        body,
        mesh=mesh,
        in_specs=placed,
        out_specs=(
            P(("groups", "fsdp"), "rows", None, None),
            P(("groups", "fsdp"), "rows", None, None),
            P(("groups", "fsdp", "rows"), None),
            P(("groups", "fsdp", "rows"), None),
        ),
        check_vma=False,
    )
```
